32 devices in a mesh: shard: 8 (over z, x), tensor: 4 (over y, core).
Axes of the slice: x: 2, y: 2, z: 4, core: 2. Of those that a mesh axis runs over, the one named last changes fastest.
Arguments:
- tokens: bfloat16 [8192, 1024], P('shard'), may hold values from -6 to 6
- cotangent: bfloat16 [8192, 1024], P('shard'), may hold values from -6 to 6
- ln_gain: bfloat16 [2, 2, 1024], P(None, None, 'shard'), may hold values from 0.25 to 1.75
- ln_bias: bfloat16 [2, 2, 1024], P(None, None, 'shard'), may hold values from -1.75 to 1.75
- w_qkv: bfloat16 [2, 1024, 3072], P(None, 'shard', 'tensor'), may hold values from -0.25 to 0.25
- b_qkv: bfloat16 [2, 3072], P(None, ('tensor', 'shard')), may hold values from -1.75 to 1.75
- w_dense: bfloat16 [2, 1024, 1024], P(None, 'tensor', 'shard'), may hold values from -0.5 to 0.5
- b_dense: bfloat16 [2, 1024], P(None, 'shard'), may hold values from -1.75 to 1.75
- w_fc1: bfloat16 [2, 1024, 4096], P(None, 'shard', 'tensor'), may hold values from -0.1875 to 0.1875
- b_fc1: bfloat16 [2, 4096], P(None, ('tensor', 'shard')), may hold values from -1.75 to 1.75
- w_fc2: bfloat16 [2, 4096, 1024], P(None, 'tensor', 'shard'), may hold values from -0.125 to 0.125
- b_fc2: bfloat16 [2, 1024], P(None, 'shard'), may hold values from -1.75 to 1.75
Outputs:
- output: bfloat16 [8192, 1024], P('shard')
- d_tokens: bfloat16 [8192, 1024], P('shard')
- d_ln_gain: float32 [2, 2, 1024], P(None, None, 'shard')
- d_ln_bias: float32 [2, 2, 1024], P(None, None, 'shard')
- d_w_qkv: float32 [2, 1024, 3072], P(None, 'shard', 'tensor')
- d_b_qkv: float32 [2, 3072], P(None, ('tensor', 'shard'))
- d_w_dense: float32 [2, 1024, 1024], P(None, 'tensor', 'shard')
- d_b_dense: float32 [2, 1024], P(None, 'shard')
- d_w_fc1: float32 [2, 1024, 4096], P(None, 'shard', 'tensor')
- d_b_fc1: float32 [2, 4096], P(None, ('tensor', 'shard'))
- d_w_fc2: float32 [2, 4096, 1024], P(None, 'tensor', 'shard')
- d_b_fc2: float32 [2, 1024], P(None, 'shard')
The draws below stay inside these ranges and needn't reach their ends.
All inputs are finite; a program needn't handle non-finite values.
Results may differ from the reference program's by a relative error of at most 0.04.
Values may be sent and summed in bfloat16 or wider, within the bound.
No kernel may reach another device: no remote copies, remote signals or barrier semaphores. Data moves between devices by JAX's collectives and lax.ppermute only.
A program may use at most 192 MiB of HBM per device.

```python
import math
import jax
import jax.numpy as jnp
from jax import lax

D = 1024
HEADS = 16
HD = 64
ROT = 16
FF = 4096
LAYERS = 2
LEN = 512
SEQ_DEV = 2
TOKENS = 8192


def steps_of(rng, dims, cuts, smallest, top_value):
    factor_of = 1.0
    for axis_at, shards_of in cuts:
        steps = jax.random.uniform(jax.random.fold_in(jax.random.fold_in(rng, 6), axis_at), (shards_of,), jnp.float32, smallest / len(cuts), top_value / len(cuts))
        factor_of = factor_of * jnp.repeat(jnp.exp(steps), dims[axis_at] // shards_of).reshape((-1,) + (1,) * (len(dims) - 1 - axis_at))
    return factor_of


def gaussian(rng, shape, width, limit, shards=(), held_as=jnp.bfloat16):
    values = width * jax.random.normal(rng, shape, jnp.float32)
    if shards:
        values = values * steps_of(rng, shape, shards, -0.22, 0.18)
    return jnp.clip(values, -limit, limit).astype(held_as)


def setup_inputs(seed: int = 0) -> dict:
    splits = jax.random.split(jax.random.key(seed), 13)
    tokens = gaussian(splits[0], (TOKENS, D), 1.0, 6.0, ((0, 8),))
    cotangent = gaussian(splits[1], (TOKENS, D), 1.0, 6.0, ((0, 8),))
    ln_gain = jnp.clip(1.0 + 0.15 * jax.random.normal(splits[2], (LAYERS, 2, D), jnp.float32), 0.25, 1.75).astype(jnp.bfloat16)
    ln_bias = gaussian(splits[3], (LAYERS, 2, D), 0.3, 1.75, ((2, 8),))
    w_qkv = gaussian(splits[4], (LAYERS, D, 3 * D), (D // 2) ** -0.5, 0.25, ((1, 8), (2, 4)))
    b_qkv = gaussian(splits[5], (LAYERS, 3 * D), 0.3, 1.75, ((1, 32),))
    w_dense = gaussian(splits[6], (LAYERS, D, D), (D // 8) ** -0.5, 0.5, ((1, 4), (2, 8)))
    b_dense = gaussian(splits[7], (LAYERS, D), 0.3, 1.75, ((1, 8),))
    w_fc1 = gaussian(splits[8], (LAYERS, D, FF), D ** -0.5, 0.1875, ((1, 8), (2, 4)))
    b_fc1 = gaussian(splits[9], (LAYERS, FF), 0.3, 1.75, ((1, 32),))
    w_fc2 = gaussian(splits[10], (LAYERS, FF, D), (FF // 2) ** -0.5, 0.125, ((1, 4), (2, 8)))
    b_fc2 = gaussian(splits[11], (LAYERS, D), 0.3, 1.75, ((1, 8),))
    return dict(tokens=tokens, cotangent=cotangent, ln_gain=ln_gain, ln_bias=ln_bias, w_qkv=w_qkv, b_qkv=b_qkv, w_dense=w_dense, b_dense=b_dense, w_fc1=w_fc1, b_fc1=b_fc1, w_fc2=w_fc2, b_fc2=b_fc2)


@jax.custom_vjp
def low(v):
    return lax.optimization_barrier(v.astype(jnp.bfloat16)).astype(jnp.float32)

@jax.custom_vjp
def low_back(v):
    return v

def low_keep(v):
    return (low(v), None)

def low_pass(kept, grad):
    return (grad,)

def back_keep(v):
    return (v, None)

def back_low(kept, grad):
    return (low(grad),)
low.defvjp(low_keep, low_pass)
low_back.defvjp(back_keep, back_low)
HIGHEST = lax.Precision.HIGHEST

def rotate_tables(token_count):
    half = ROT // 2
    places = (jnp.arange(token_count) % LEN).astype(jnp.float32)
    freqs = jnp.exp(-(2.0 * jnp.arange(half).astype(jnp.float32) / ROT) * math.log(10000.0))
    angles = places[:, None] * freqs[None, :]
    angles = jnp.concatenate([angles, angles], axis=1)
    return (jnp.cos(angles)[:, None, :], jnp.sin(angles)[:, None, :])

def rotate(part, cosine, sine):
    inner = part[..., :ROT]
    lower = inner[..., :ROT // 2]
    upper = inner[..., ROT // 2:]
    turned = inner * cosine + jnp.concatenate([-upper, lower], axis=-1) * sine
    return jnp.concatenate([turned, part[..., ROT:]], axis=-1)

def normalize(resid):
    centered = resid - lax.optimization_barrier(jnp.mean(resid, axis=-1, keepdims=True))
    factor = lax.rsqrt(lax.optimization_barrier(jnp.mean(centered * centered, axis=-1, keepdims=True)) + 1e-05)
    return centered * factor

def attend(parts):
    queries, key_rows, value_rows = parts
    scores = jnp.einsum('bqhd,bkhd->bhqk', queries, key_rows, precision=HIGHEST) * (1.0 / math.sqrt(HD))
    scores = low_back(scores)
    causal = jnp.arange(LEN)[:, None] >= jnp.arange(LEN)[None, :]
    scores = jnp.where(causal, scores, -1e+30)
    chances = low(jax.nn.softmax(scores, axis=-1))
    return jnp.einsum('bhqk,bkhd->bqhd', chances, value_rows, precision=HIGHEST)

def block(resid, weights, cosine, sine):
    gains, biases, qkv_mat, qkv_bias, dense_mat, dense_bias, up_mat, up_bias, down_mat, down_bias = weights
    token_count = resid.shape[0]
    normed = normalize(resid)
    first = low(normed * gains[0] + biases[0])
    second = low(normed * gains[1] + biases[1])
    joined = low_back(jnp.dot(first, qkv_mat, precision=HIGHEST) + qkv_bias).reshape(token_count, HEADS, 3, HD)
    queries = low(rotate(joined[:, :, 0], cosine, sine))
    key_rows = low(rotate(joined[:, :, 1], cosine, sine))
    value_rows = low(joined[:, :, 2])
    group_rows = SEQ_DEV * LEN

    def shaped(part):
        return part.reshape(token_count // group_rows, SEQ_DEV, LEN, HEADS, HD)
    mixed = lax.map(jax.checkpoint(attend), (shaped(queries), shaped(key_rows), shaped(value_rows)))
    mixed = low(low_back(mixed.reshape(token_count, HEADS * HD)))
    hidden_in = low_back(jnp.dot(second, up_mat, precision=HIGHEST) + up_bias)
    hidden = low(jax.nn.gelu(hidden_in, approximate=False))
    branch = low_back(jnp.dot(mixed, dense_mat, precision=HIGHEST) + dense_bias + jnp.dot(hidden, down_mat, precision=HIGHEST) + down_bias)
    return resid + branch

def reference(tokens, cotangent, ln_gain, ln_bias, w_qkv, b_qkv, w_dense, b_dense, w_fc1, b_fc1, w_fc2, b_fc2):
    params = tuple((item.astype(jnp.float32) for item in (ln_gain, ln_bias, w_qkv, b_qkv, w_dense, b_dense, w_fc1, b_fc1, w_fc2, b_fc2)))
    cosine, sine = rotate_tables(tokens.shape[0])

    def forward(resid, layer_params):
        for layer in range(LAYERS):
            resid = block(resid, [item[layer] for item in layer_params], cosine, sine)
        return resid
    result, pullback = jax.vjp(forward, tokens.astype(jnp.float32), params)
    d_input, grads = pullback(cotangent.astype(jnp.float32))
    return (result.astype(jnp.bfloat16), d_input.astype(jnp.bfloat16), grads[0], grads[1], grads[2], grads[3], grads[4], grads[5], grads[6], grads[7], grads[8], grads[9])
```

```python
import math

import jax
import jax.numpy as jnp
from jax import lax
from jax.sharding import PartitionSpec as P

HD = 64
ROT = 16
LAYERS = 2
LEN = 512
BF = jnp.bfloat16
F32 = jnp.float32


def ring_order(count):
    return list(range(0, count, 2)) + list(range(count - 1, 0, -2))


def ring_perms(count):
    order = ring_order(count)
    ahead = [(order[i], order[(i + 1) % count]) for i in range(count)]
    return ahead, [(b, a) for a, b in ahead]


def after(value, *others):
    return lax.optimization_barrier((value,) + others)[0]


class Ring:
    def __init__(self):
        self.count = lax.axis_size("shard")
        self.order = ring_order(self.count)
        self.ahead, self.back = ring_perms(self.count)
        table = [0] * self.count
        for place, device in enumerate(self.order):
            table[device] = place
        me = lax.axis_index("shard")
        place = jnp.array(table, jnp.int32)[me]
        owners = jnp.array(self.order, jnp.int32)
        self.owner = [owners[(place + step) % self.count] for step in range(self.count)]
        self.me = me

    def gather(self, part, gate=None):
        count, half = self.count, part.shape[1] // 2
        whole = jnp.zeros((count,) + part.shape, part.dtype)

        def put(whole, piece, owner, col=0):
            return lax.dynamic_update_slice(whole, piece[None], (owner, 0, col))

        whole = put(whole, part, self.me)
        if gate is not None:
            part = after(part, gate)
        up = down = part
        for step in range(1, count // 2):
            up = lax.ppermute(up, "shard", self.ahead)
            down = lax.ppermute(down, "shard", self.back)
            whole = put(whole, up, self.owner[count - step])
            whole = put(whole, down, self.owner[step])
        gate = (up, down)
        left = lax.ppermute(up[:, :half], "shard", self.ahead)
        right = lax.ppermute(down[:, half:], "shard", self.back)
        far = count // 2
        whole = put(whole, left, self.owner[far])
        whole = put(whole, right, self.owner[far], half)
        return whole.reshape(count * part.shape[0], part.shape[1]), gate

    def scatter(self, total, gate=None):
        count = self.count
        rows, cols = total.shape[0] // count, total.shape[1]
        half = cols // 2

        def piece(step, lo=0, hi=None):
            hi = cols if hi is None else hi
            return lax.dynamic_slice(total, (self.owner[step % count] * rows, lo), (rows, hi - lo))

        far = count // 2
        head_up, head_down = piece(far, 0, half), piece(far, half, cols)
        if gate is not None:
            head_up, head_down = after(head_up, gate), after(head_down, gate)
        head_up = lax.ppermute(head_up, "shard", self.ahead)
        head_down = lax.ppermute(head_down, "shard", self.back)
        up = jnp.concatenate(
            [
                (piece(far - 1, 0, half).astype(F32) + head_up.astype(F32)).astype(BF),
                piece(far - 1, half, cols),
            ],
            axis=1,
        )
        down = jnp.concatenate(
            [
                piece(far + 1, 0, half),
                (piece(far + 1, half, cols).astype(F32) + head_down.astype(F32)).astype(BF),
            ],
            axis=1,
        )
        for step in range(far - 1, 0, -1):
            up = lax.ppermute(up, "shard", self.ahead)
            down = lax.ppermute(down, "shard", self.back)
            if step > 1:
                up = (up.astype(F32) + piece(step - 1).astype(F32)).astype(BF)
                down = (down.astype(F32) + piece(count - step + 1).astype(F32)).astype(BF)
        return up.astype(F32) + down.astype(F32) + piece(0).astype(F32), (up, down)

    def small_sum(self, value):
        total = value
        for step in range(1, self.count):
            perm = [(i, (i + step) % self.count) for i in range(self.count)]
            total = total + lax.ppermute(value, "shard", perm)
        return total


def partner(bit):
    count = lax.axis_size("tensor")
    return [(i, i ^ (1 << bit)) for i in range(count)]


def tensor_bits():
    return lax.axis_size("tensor").bit_length() - 1


def tensor_scatter(part):
    me = lax.axis_index("tensor")
    for bit in range(tensor_bits()):
        rows = part.shape[0] // 2
        side = (me >> bit) & 1
        keep = lax.dynamic_slice_in_dim(part, side * rows, rows, 0)
        give = lax.dynamic_slice_in_dim(part, (1 - side) * rows, rows, 0)
        got = lax.ppermute(give.astype(BF), "tensor", partner(bit))
        part = keep.astype(F32) + got.astype(F32)
    return part


def tensor_own(part):
    me = lax.axis_index("tensor")
    for bit in range(tensor_bits()):
        rows = part.shape[0] // 2
        part = lax.dynamic_slice_in_dim(part, ((me >> bit) & 1) * rows, rows, 0)
    return part


def tensor_gather(part):
    me = lax.axis_index("tensor")
    for bit in reversed(range(tensor_bits())):
        got = lax.ppermute(part, "tensor", partner(bit))
        side = (me >> bit) & 1
        part = jnp.where(
            side == 0, jnp.concatenate([part, got], axis=0), jnp.concatenate([got, part], axis=0)
        )
    return part


def tensor_small_sum(value):
    for bit in range(tensor_bits()):
        value = value + lax.ppermute(value, "tensor", partner(bit))
    return value


def rotate_tables():
    half = ROT // 2
    places = jnp.arange(LEN).astype(F32)
    freqs = jnp.exp(-(2.0 * jnp.arange(half).astype(F32) / ROT) * math.log(10000.0))
    angles = places[:, None] * freqs[None, :]
    angles = jnp.concatenate([angles, angles], axis=1)
    return (jnp.cos(angles)[:, None, :], jnp.sin(angles)[:, None, :])


def rotate(part, cosine, sine):
    inner = part[..., :ROT]
    lower = inner[..., : ROT // 2]
    upper = inner[..., ROT // 2 :]
    turned = inner * cosine + jnp.concatenate([-upper, lower], axis=-1) * sine
    return jnp.concatenate([turned, part[..., ROT:]], axis=-1)


def rotate_back(grad, cosine, sine):
    inner = grad[..., :ROT]
    scaled = inner * sine
    lower = scaled[..., : ROT // 2]
    upper = scaled[..., ROT // 2 :]
    turned = inner * cosine + jnp.concatenate([upper, -lower], axis=-1)
    return jnp.concatenate([turned, grad[..., ROT:]], axis=-1)


def attend(joined, tables):
    heads = joined.shape[1] // (3 * HD)
    joined = joined.reshape(LEN, 3, heads, HD)
    queries = rotate(joined[:, 0], *tables).astype(BF)
    key_rows = rotate(joined[:, 1], *tables).astype(BF)
    value_rows = joined[:, 2].astype(BF)
    scores = jnp.einsum("qhd,khd->hqk", queries, key_rows, preferred_element_type=F32)
    scores = scores * (1.0 / math.sqrt(HD))
    causal = jnp.arange(LEN)[:, None] >= jnp.arange(LEN)[None, :]
    scores = jnp.where(causal, scores, -1e30)
    highest = jnp.max(scores, axis=-1, keepdims=True)
    log_total = highest + jnp.log(jnp.sum(jnp.exp(scores - highest), axis=-1, keepdims=True))
    chances = jnp.exp(scores - log_total).astype(BF)
    mixed = jnp.einsum("hqk,khd->qhd", chances, value_rows, preferred_element_type=F32)
    return mixed.astype(BF).reshape(LEN, heads * HD), (queries, key_rows, value_rows, log_total)


def attend_back(d_mixed, kept, tables):
    queries, key_rows, value_rows, log_total = kept
    heads = queries.shape[1]
    scores = jnp.einsum("qhd,khd->hqk", queries, key_rows, preferred_element_type=F32)
    scores = scores * (1.0 / math.sqrt(HD))
    causal = jnp.arange(LEN)[:, None] >= jnp.arange(LEN)[None, :]
    chances = jnp.exp(jnp.where(causal, scores, -1e30) - log_total)
    d_mixed = d_mixed.reshape(LEN, heads, HD)
    d_value = jnp.einsum("hqk,qhd->khd", chances.astype(BF), d_mixed, preferred_element_type=F32)
    d_chances = jnp.einsum("qhd,khd->hqk", d_mixed, value_rows, preferred_element_type=F32)
    row_inner = jnp.sum(chances * d_chances, axis=-1, keepdims=True)
    d_scores = (chances * (d_chances - row_inner)).astype(BF)
    scale = 1.0 / math.sqrt(HD)
    d_query = jnp.einsum("hqk,khd->qhd", d_scores, key_rows, preferred_element_type=F32) * scale
    d_key = jnp.einsum("hqk,qhd->khd", d_scores, queries, preferred_element_type=F32) * scale
    d_joined = jnp.stack(
        [rotate_back(d_query, *tables), rotate_back(d_key, *tables), d_value], axis=1
    )
    return d_joined.astype(BF).reshape(LEN, 3 * heads * HD)


def normalize(resid):
    centered = resid - jnp.mean(resid, axis=-1, keepdims=True)
    factor = lax.rsqrt(jnp.mean(centered * centered, axis=-1, keepdims=True) + 1e-05)
    return (centered * factor, factor)


def gelu_both(hidden_in):
    normal_cdf = 0.5 * (1.0 + jax.scipy.special.erf(hidden_in * (1.0 / math.sqrt(2.0))))
    density = jnp.exp(-0.5 * hidden_in * hidden_in) * (1.0 / math.sqrt(2.0 * math.pi))
    return hidden_in * normal_cdf, normal_cdf + hidden_in * density


def by_kind(mat):
    lead, cols = mat.shape[:-1], mat.shape[-1]
    mat = mat.reshape(lead + (cols // (3 * HD), 3, HD))
    return jnp.swapaxes(mat, -3, -2).reshape(lead + (cols,))


def by_head(mat):
    lead, cols = mat.shape[:-1], mat.shape[-1]
    mat = mat.reshape(lead + (3, cols // (3 * HD), HD))
    return jnp.swapaxes(mat, -3, -2).reshape(lead + (cols,))


def per_device(
    tokens, cotangent, ln_gain, ln_bias, w_qkv, b_qkv, w_dense, b_dense, w_fc1, b_fc1, w_fc2, b_fc2
):
    streams = tokens.shape[0] // LEN
    model = tokens.shape[1]
    qkv_cols, ff_cols = w_qkv.shape[2], w_fc1.shape[2]
    mix_cols = qkv_cols // 3
    in_cols = qkv_cols + ff_cols
    ring = Ring()
    count, me = ring.count, ring.me
    tables = rotate_tables()
    gains, shifts = ln_gain.astype(F32), ln_bias.astype(F32)

    raw_in, parts_qkv, parts_up, parts_out, smalls = [], [], [], [], []
    for layer in range(LAYERS):
        raw = jnp.concatenate([by_kind(w_qkv[layer]), w_fc1[layer]], axis=1).astype(F32)
        raw_in.append(raw)
        gain = jnp.concatenate(
            [
                jnp.broadcast_to(gains[layer, k][:, None], (raw.shape[0], width))
                for k, width in ((0, qkv_cols), (1, ff_cols))
            ],
            axis=1,
        )
        scaled = (raw * gain).astype(BF)
        parts_qkv.append(scaled[:, :qkv_cols])
        parts_up.append(scaled[:, qkv_cols:])
        parts_out.append(
            jnp.concatenate([w_dense[layer].T, w_fc2[layer].T], axis=1)
        )
        moved = jnp.concatenate(
            [
                jnp.sum(raw[:, :qkv_cols] * shifts[layer, 0][:, None], axis=0),
                jnp.sum(raw[:, qkv_cols:] * shifts[layer, 1][:, None], axis=0),
            ]
        )
        own = jnp.zeros((qkv_cols,), F32)
        own = lax.dynamic_update_slice(
            own, b_qkv[layer].astype(F32), (me * b_qkv.shape[1],)
        )
        own_up = lax.dynamic_update_slice(
            jnp.zeros((ff_cols,), F32), b_fc1[layer].astype(F32), (me * b_fc1.shape[1],)
        )
        own_out = lax.dynamic_update_slice(
            jnp.zeros((model,), F32),
            b_dense[layer].astype(F32) + b_fc2[layer].astype(F32),
            (me * b_dense.shape[1],),
        )
        smalls.append(
            jnp.concatenate([moved + jnp.concatenate([by_kind(own), own_up]), own_out])
        )
    biases = ring.small_sum(jnp.stack(smalls))

    gate = None
    mats = []
    for layer in range(LAYERS):
        qkv_mat, gate = ring.gather(parts_qkv[layer], gate)
        up_mat, gate = ring.gather(parts_up[layer], gate)
        out_mat, gate = ring.gather(parts_out[layer], gate)
        mats.append((qkv_mat, up_mat, out_mat))

    token_streams = [tokens[i * LEN : (i + 1) * LEN].astype(F32) for i in range(streams)]
    resid = [tensor_own(item) for item in token_streams]
    stored = [[None] * streams for _ in range(LAYERS)]
    outputs = []
    for layer in range(LAYERS):
        qkv_mat, up_mat, out_mat = mats[layer]
        for i in range(streams):
            own_normed, factor = normalize(resid[i])
            if layer == 0:
                normed = normalize(token_streams[i])[0].astype(BF)
            else:
                normed = tensor_gather(own_normed.astype(BF))
            joined = (
                jnp.dot(normed, qkv_mat, preferred_element_type=F32) + biases[layer, :qkv_cols]
            )
            mixed, kept = attend(joined, tables)
            hidden_in = (
                jnp.dot(normed, up_mat, preferred_element_type=F32)
                + biases[layer, qkv_cols:in_cols]
            )
            hidden, slope = gelu_both(hidden_in)
            hidden, slope = hidden.astype(BF), slope.astype(BF)
            both = jnp.concatenate([mixed, hidden], axis=1)
            partial = lax.dot_general(
                both, out_mat, (((1,), (1,)), ((), ())), preferred_element_type=F32
            ).astype(BF)
            branch = tensor_scatter(partial) + biases[layer, in_cols:]
            stored[layer][i] = (normed, own_normed, factor, kept, slope, both)
            resid[i] = resid[i] + branch
    for i in range(streams):
        outputs.append(tensor_gather(resid[i].astype(BF)))

    cotangent_streams = [cotangent[i * LEN : (i + 1) * LEN] for i in range(streams)]
    grad = [tensor_own(item).astype(F32) for item in cotangent_streams]
    grad_low = cotangent_streams
    gate = None
    in_grads, out_grads, small_grads = [None] * LAYERS, [None] * LAYERS, [None] * LAYERS
    for layer in reversed(range(LAYERS)):
        qkv_mat, up_mat, out_mat = mats[layer]
        low = jnp.concatenate(grad_low, axis=0)
        both = jnp.concatenate([item[5] for item in stored[layer]], axis=0)
        d_out = lax.dot_general(
            low, both, (((0,), (0,)), ((), ())), preferred_element_type=F32
        ).astype(BF)
        out_grads[layer], gate = ring.scatter(d_out, gate)
        d_ins = []
        for i in range(streams):
            normed, own_normed, factor, kept, slope, _ = stored[layer][i]
            d_both = jnp.dot(grad_low[i], out_mat, preferred_element_type=F32)
            d_mixed = d_both[:, :mix_cols].astype(BF)
            d_hidden_in = (d_both[:, mix_cols:] * slope.astype(F32)).astype(BF)
            d_joined = attend_back(d_mixed, kept, tables)
            d_in = jnp.concatenate([d_joined, d_hidden_in], axis=1)
            d_ins.append(d_in)
            in_mat = jnp.concatenate([qkv_mat, up_mat], axis=1)
            shaped = lax.dot_general(
                d_in, in_mat, (((1,), (1,)), ((), ())), preferred_element_type=F32
            ).astype(BF)
            shaped = tensor_scatter(shaped)
            grad[i] = grad[i] + factor * (
                shaped
                - jnp.mean(shaped, axis=-1, keepdims=True)
                - own_normed * jnp.mean(shaped * own_normed, axis=-1, keepdims=True)
            )
        d_in = jnp.concatenate(d_ins, axis=0)
        normed = jnp.concatenate([item[0] for item in stored[layer]], axis=0)
        d_in_mat = lax.dot_general(
            normed, d_in, (((0,), (0,)), ((), ())), preferred_element_type=F32
        ).astype(BF)
        in_grads[layer], gate = ring.scatter(d_in_mat, gate)
        small_grads[layer] = jnp.concatenate(
            [jnp.sum(d_in.astype(F32), axis=0), jnp.sum(low.astype(F32), axis=0)]
        )
        grad_low = [tensor_gather(item.astype(BF)) for item in grad]

    d_tokens = jnp.concatenate(grad_low, axis=0)
    output = jnp.concatenate(outputs, axis=0)
    sums = [ring.small_sum(item) for item in small_grads]

    results = []
    norm_sums = []
    for layer in range(LAYERS):
        grads, sum_in, raw = in_grads[layer], sums[layer][:in_cols], raw_in[layer]
        weighted, moved = raw * grads, raw * sum_in[None, :]
        norm_sums.append(
            jnp.stack(
                [
                    jnp.sum(weighted[:, :qkv_cols], axis=1),
                    jnp.sum(weighted[:, qkv_cols:], axis=1),
                    jnp.sum(moved[:, :qkv_cols], axis=1),
                    jnp.sum(moved[:, qkv_cols:], axis=1),
                ]
            )
        )
        d_qkv = (
            gains[layer, 0][:, None] * grads[:, :qkv_cols]
            + shifts[layer, 0][:, None] * sum_in[None, :qkv_cols]
        )
        d_up = (
            gains[layer, 1][:, None] * grads[:, qkv_cols:]
            + shifts[layer, 1][:, None] * sum_in[None, qkv_cols:]
        )
        d_qkv_bias = by_head(sum_in[:qkv_cols])
        results.append(
            (
                by_head(d_qkv),
                lax.dynamic_slice(d_qkv_bias, (me * b_qkv.shape[1],), (b_qkv.shape[1],)),
                out_grads[layer][:, :mix_cols].T,
                lax.dynamic_slice(
                    sums[layer], (in_cols + me * b_dense.shape[1],), (b_dense.shape[1],)
                ),
                d_up,
                lax.dynamic_slice(
                    sums[layer], (qkv_cols + me * b_fc1.shape[1],), (b_fc1.shape[1],)
                ),
                out_grads[layer][:, mix_cols:].T,
            )
        )
    norm_sums = tensor_small_sum(jnp.stack(norm_sums))

    def stacked(index):
        return jnp.stack([results[layer][index] for layer in range(LAYERS)])

    return (
        output,
        d_tokens,
        norm_sums[:, :2],
        norm_sums[:, 2:],
        stacked(0),
        stacked(1),
        stacked(2),
        stacked(3),
        stacked(4),
        stacked(5),
        stacked(6),
        stacked(3),
    )


def solution(mesh):
    in_specs = (
        P("shard", None),
        P("shard", None),
        P(None, None, "shard"),
        P(None, None, "shard"),
        P(None, "shard", "tensor"),
        P(None, ("tensor", "shard")),
        P(None, "tensor", "shard"),
        P(None, "shard"),
        P(None, "shard", "tensor"),
        P(None, ("tensor", "shard")),
        P(None, "tensor", "shard"),
        P(None, "shard"),
    )
    out_specs = (
        P("shard", None),
        P("shard", None),
        P(None, None, "shard"),
        P(None, None, "shard"),
        P(None, "shard", "tensor"),
        P(None, ("tensor", "shard")),
        P(None, "tensor", "shard"),
        P(None, "shard"),
        P(None, "shard", "tensor"),
        P(None, ("tensor", "shard")),
        P(None, "tensor", "shard"),
        P(None, "shard"),
    )
    return jax.shard_map(
        per_device, mesh=mesh, in_specs=in_specs, out_specs=out_specs, check_vma=False
    )
```

```python
import functools
import math

import jax
import jax.numpy as jnp
from jax import lax
from jax.experimental import pallas as pl
from jax.experimental.pallas import tpu as pltpu
from jax.sharding import PartitionSpec as P

HD = 64
ROT = 16
LAYERS = 2
LEN = 512
EXTRA = 16
BF = jnp.bfloat16
F32 = jnp.float32
NT = (((1,), (1,)), ((), ()))
TN = (((0,), (0,)), ((), ()))
VMEM_LIMIT = 56 * 1024 * 1024


def shape(dims, dtype=BF):
    return jax.ShapeDtypeStruct(dims, dtype)


def whole(dims):
    return pl.BlockSpec(dims, lambda *_: (0,) * len(dims))


def call(kernel, out_shape, grid=None, flops=0, moved=0, **kw):
    params = pltpu.CompilerParams(vmem_limit_bytes=VMEM_LIMIT)
    cost = pl.CostEstimate(flops=int(flops), bytes_accessed=int(moved), transcendentals=0)
    if grid is not None:
        kw["grid"] = grid
    return pl.pallas_call(
        kernel, out_shape=out_shape, compiler_params=params, cost_estimate=cost, **kw
    )


def ring_order(count):
    return list(range(0, count, 2)) + list(range(count - 1, 0, -2))


def ring_perms(count):
    order = ring_order(count)
    ahead = [(order[i], order[(i + 1) % count]) for i in range(count)]
    return ahead, [(b, a) for a, b in ahead]


def after(value, *others):
    return lax.optimization_barrier((value,) + others)[0]


def assemble_kernel(count, rows, owner, *refs):
    pieces, out, rest = refs[: count + 1], refs[count + 1], refs[count + 2 :]
    half = out.shape[2] // 2
    far = count // 2
    for step in range(count):
        if step == far:
            continue
        piece = pieces[step if step < far else step + 1]
        out[owner[step]] = piece[:rows]
    out[owner[far], :, :half] = pieces[far][:rows]
    out[owner[far], :, half:] = pieces[far + 1][:rows]
    if rest:
        tail = pieces[0][rows:].astype(F32)
        for step in range(1, count):
            if step != far:
                tail = tail + pieces[step if step < far else step + 1][rows:].astype(F32)
        other = jnp.concatenate([pieces[far][rows:], pieces[far + 1][rows:]], axis=1)
        rest[0][...] = tail + other.astype(F32)


def add_first_kernel(_, left, right, up_piece, down_piece, up, down):
    half = left.shape[1]
    up[:, :half] = (up_piece[0, :, :half].astype(F32) + left[...].astype(F32)).astype(BF)
    up[:, half:] = up_piece[0, :, half:]
    down[:, :half] = down_piece[0, :, :half]
    down[:, half:] = (down_piece[0, :, half:].astype(F32) + right[...].astype(F32)).astype(BF)


def add_kernel(_, up_in, down_in, up_piece, down_piece, up, down):
    up[...] = (up_piece[0].astype(F32) + up_in[...].astype(F32)).astype(BF)
    down[...] = (down_piece[0].astype(F32) + down_in[...].astype(F32)).astype(BF)


def add_last_kernel(_, up_in, down_in, piece, out):
    out[...] = piece[0].astype(F32) + (up_in[...].astype(F32) + down_in[...].astype(F32))


class Ring:
    def __init__(self):
        self.count = lax.axis_size("shard")
        self.order = ring_order(self.count)
        self.ahead, self.back = ring_perms(self.count)
        table = [0] * self.count
        for place, device in enumerate(self.order):
            table[device] = place
        me = lax.axis_index("shard")
        place = jnp.array(table, jnp.int32)[me]
        steps = jnp.arange(self.count, dtype=jnp.int32)
        self.owner = jnp.array(self.order, jnp.int32)[(place + steps) % self.count]
        self.me = me

    def gather(self, part, rows, gate=None):
        count, cols = self.count, part.shape[1]
        half, far = cols // 2, self.count // 2
        if gate is not None:
            part = after(part, gate)
        up = down = part
        pieces = [part] + [None] * count
        for step in range(1, far):
            up = lax.ppermute(up, "shard", self.ahead)
            down = lax.ppermute(down, "shard", self.back)
            pieces[count + 1 - step] = up
            pieces[step] = down
        gate = (up, down)
        pieces[far] = lax.ppermute(up[:, :half], "shard", self.ahead)
        pieces[far + 1] = lax.ppermute(down[:, half:], "shard", self.back)
        outs = [shape((count, rows, cols))]
        if part.shape[0] > rows:
            outs.append(shape((part.shape[0] - rows, cols), F32))
        result = call(
            functools.partial(assemble_kernel, count, rows),
            outs,
            moved=4 * count * rows * cols,
            in_specs=[pl.BlockSpec(memory_space=pltpu.SMEM)]
            + [pl.BlockSpec(memory_space=pltpu.VMEM)] * (count + 1),
        )(self.owner, *pieces)
        return [result[0].reshape(count * rows, cols)] + list(result[1:]), gate

    def scatter(self, total):
        count, rows, cols = total.shape
        half, far = cols // 2, count // 2

        def add(kernel, ups, chosen, outs):
            def place(which):
                return pl.BlockSpec((1, rows, cols), lambda i, own: (own[which], 0, 0))

            return pl.pallas_call(
                kernel,
                out_shape=outs,
                grid_spec=pltpu.PrefetchScalarGridSpec(
                    num_scalar_prefetch=1,
                    grid=(1,),
                    in_specs=[whole(item.shape) for item in ups] + [place(c) for c in chosen],
                    out_specs=[whole(item.shape) for item in outs],
                ),
                compiler_params=pltpu.CompilerParams(vmem_limit_bytes=VMEM_LIMIT),
                cost_estimate=pl.CostEstimate(
                    flops=0, bytes_accessed=12 * rows * cols, transcendentals=0
                ),
            )(self.owner, *ups, *([total] * len(chosen)))

        head = lax.dynamic_index_in_dim(total, self.owner[far], 0, False)
        left = lax.ppermute(head[:, :half], "shard", self.ahead)
        right = lax.ppermute(head[:, half:], "shard", self.back)
        pair = [shape((rows, cols))] * 2
        up, down = add(add_first_kernel, (left, right), (far - 1, far + 1), pair)
        for step in range(far - 1, 0, -1):
            up = lax.ppermute(up, "shard", self.ahead)
            down = lax.ppermute(down, "shard", self.back)
            if step > 1:
                up, down = add(add_kernel, (up, down), (step - 1, count - step + 1), pair)
        return add(add_last_kernel, (up, down), (0,), [shape((rows, cols), F32)])[0]


def partner(bit):
    count = lax.axis_size("tensor")
    return [(i, i ^ (1 << bit)) for i in range(count)]


def tensor_bits():
    return lax.axis_size("tensor").bit_length() - 1


def tensor_scatter(part):
    me = lax.axis_index("tensor")
    for bit in range(tensor_bits()):
        rows = part.shape[0] // 2
        side = (me >> bit) & 1
        keep = lax.dynamic_slice_in_dim(part, side * rows, rows, 0)
        give = lax.dynamic_slice_in_dim(part, (1 - side) * rows, rows, 0)
        got = lax.ppermute(give.astype(BF), "tensor", partner(bit))
        part = keep.astype(F32) + got.astype(F32)
    return part[0]


def tensor_own(part):
    me = lax.axis_index("tensor")
    for bit in range(tensor_bits()):
        rows = part.shape[0] // 2
        part = lax.dynamic_slice_in_dim(part, ((me >> bit) & 1) * rows, rows, 0)
    return part[0]


def tensor_gather(part):
    me = lax.axis_index("tensor")
    part = part[None]
    for bit in reversed(range(tensor_bits())):
        got = lax.ppermute(part, "tensor", partner(bit))
        side = (me >> bit) & 1
        part = jnp.where(
            side == 0, jnp.concatenate([part, got], axis=0), jnp.concatenate([got, part], axis=0)
        )
    return part


def tensor_small_sum(value):
    for bit in range(tensor_bits()):
        value = value + lax.ppermute(value, "tensor", partner(bit))
    return value


def rotate_tables():
    half = ROT // 2
    places = jnp.arange(LEN).astype(F32)
    freqs = jnp.exp(-(2.0 * jnp.arange(half).astype(F32) / ROT) * math.log(10000.0))
    angles = freqs[:, None] * places[None, :]
    return jnp.cos(angles), jnp.sin(angles)


def column(row):
    return jnp.transpose(jnp.broadcast_to(row, (8, row.shape[1])))[:, :1]


def pack_kernel(norms, own, w_qkv, w_up, w_dense, w_down, *outs):
    heads = w_qkv.shape[2] // (3 * HD)
    qkv_cols, up_cols = w_qkv.shape[2], w_up.shape[2]
    mix_cols = qkv_cols // 3
    rows = w_qkv.shape[1]
    tail = []
    for layer in range(LAYERS):
        raw = w_qkv[layer]
        by_kind = jnp.concatenate(
            [
                raw[:, (h * 3 + kind) * HD : (h * 3 + kind + 1) * HD]
                for kind in range(3)
                for h in range(heads)
            ],
            axis=1,
        )
        up = w_up[layer]
        gains = [column(norms[2 * layer + k : 2 * layer + k + 1, :]) for k in range(2)]
        shifts = [norms[4 + 2 * layer + k : 5 + 2 * layer + k, :] for k in range(2)]
        scaled = [
            (mat.astype(F32) * gain).astype(BF) for mat, gain in zip((by_kind, up), gains)
        ]
        moved = [
            jnp.dot(
                jnp.broadcast_to(row, (16, rows)).astype(BF), mat, preferred_element_type=F32
            )[:1]
            for mat, row in zip((by_kind, up), shifts)
        ]
        total = own[layer : layer + 1, :]
        pad = total.shape[1] - qkv_cols - up_cols
        total = total + jnp.concatenate(moved + [jnp.zeros((1, pad), F32)], axis=1)
        high = total.astype(BF).astype(F32)
        for value in (high, total - high):
            for at in range(0, total.shape[1], qkv_cols):
                tail.append(value[:, at : at + qkv_cols])
        if layer == 0:
            outs[0][:rows, :] = scaled[0]
            outs[1][...] = scaled[1]
        else:
            outs[3][:, :qkv_cols] = scaled[0]
            outs[3][:, qkv_cols:] = scaled[1]
        out = outs[2] if layer == 0 else outs[4]
        out[:, :mix_cols] = w_dense[layer].astype(F32).T.astype(BF)
        out[:, mix_cols:] = w_down[layer].astype(F32).T.astype(BF)
    outs[0][rows:, :] = jnp.concatenate(tail, axis=0).astype(BF)


def attend_kernel(x, mat, bias, cosine, sine, qkv, mixed, log_total, turned):
    @pl.when(pl.program_id(0) == 0)
    def _():
        turned[...] = mat[:, : turned.shape[0]].T

    seq = jnp.concatenate([x[b] for b in range(x.shape[0])], axis=1)
    joined = jnp.dot(turned[...], seq, preferred_element_type=F32) + column(bias[...])
    part = joined.shape[0] // 3
    heads = part // HD
    half = ROT // 2
    cos, sin = cosine[...], sine[...]
    for kind in range(2):
        for h in range(heads):
            at = kind * part + h * HD
            low, high = joined[at : at + half], joined[at + half : at + ROT]
            turn = jnp.concatenate([low * cos - high * sin, high * cos + low * sin], axis=0)
            qkv[at : at + ROT, :] = turn.astype(BF)
            qkv[at + ROT : at + HD, :] = joined[at + ROT : at + HD].astype(BF)
    qkv[2 * part :, :] = joined[2 * part :].astype(BF)
    wide = LEN // 2
    log_total[...] = jnp.zeros_like(log_total)
    for h in range(heads):
        for q_at in range(0, LEN, wide):
            keys = q_at + wide
            query = qkv[h * HD : (h + 1) * HD, q_at:keys]
            key = qkv[part + h * HD : part + (h + 1) * HD, :keys]
            value = qkv[2 * part + h * HD : 2 * part + (h + 1) * HD, :keys]
            scores = masked_scores(key, query, q_at)
            highest = jnp.max(scores, axis=0, keepdims=True)
            chances = jnp.exp(scores - highest)
            total = jnp.sum(chances, axis=0, keepdims=True)
            out = jnp.dot(value, chances.astype(BF), preferred_element_type=F32)
            for b in range(wide // mixed.shape[2]):
                cut = slice(b * mixed.shape[2], (b + 1) * mixed.shape[2])
                at = q_at // mixed.shape[2] + b
                mixed[at, h * HD : (h + 1) * HD, :] = (out / total)[:, cut].astype(BF)
            log_total[h : h + 1, q_at:keys] = highest + jnp.log(total)


def masked_scores(key, query, q_at):
    scores = lax.dot_general(key, query, TN, preferred_element_type=F32) * (1.0 / math.sqrt(HD))
    key_at = lax.broadcasted_iota(jnp.int32, scores.shape, 0)
    query_at = lax.broadcasted_iota(jnp.int32, scores.shape, 1) + q_at
    return jnp.where(query_at >= key_at, scores, -1e30)


def attend_back_kernel(qkv, log_total, d_mixed, cosine, sine, d_joined, grads):
    part = qkv.shape[0] // 3
    heads = part // HD
    half = ROT // 2
    wide = LEN // 2
    block = d_mixed.shape[2]
    scale = 1.0 / math.sqrt(HD)
    cos, sin = cosine[...], sine[...]
    for h in range(heads):
        d_key, d_value = [], []
        for q_at in range(0, LEN, wide):
            keys = q_at + wide
            query = qkv[h * HD : (h + 1) * HD, q_at:keys]
            key = qkv[part + h * HD : part + (h + 1) * HD, :keys]
            value = qkv[2 * part + h * HD : 2 * part + (h + 1) * HD, :keys]
            d_out = jnp.concatenate(
                [
                    d_mixed[q_at // block + b, h * HD : (h + 1) * HD, :]
                    for b in range(wide // block)
                ],
                axis=1,
            )
            scores = masked_scores(key, query, q_at)
            chances = jnp.exp(scores - log_total[h : h + 1, q_at:keys])
            d_chances = lax.dot_general(value, d_out, TN, preferred_element_type=F32)
            weighted = chances * d_chances
            inner = jnp.sum(weighted, axis=0, keepdims=True)
            d_scores = (weighted - chances * inner).astype(BF)
            grads[h * HD : (h + 1) * HD, q_at:keys] = (
                jnp.dot(key, d_scores, preferred_element_type=F32) * scale
            )
            d_key.append(lax.dot_general(query, d_scores, NT, preferred_element_type=F32))
            d_value.append(
                lax.dot_general(d_out, chances.astype(BF), NT, preferred_element_type=F32)
            )
        for base, items, factor in ((part, d_key, scale), (2 * part, d_value, 1.0)):
            at = base + h * HD
            grads[at : at + HD, :wide] = (items[0] + items[1][:, :wide]) * factor
            grads[at : at + HD, wide:] = items[1][:, wide:] * factor
    whole_grad = grads[...]
    pieces = []
    for kind in range(2):
        for h in range(heads):
            at = kind * part + h * HD
            low, high = whole_grad[at : at + half], whole_grad[at + half : at + ROT]
            pieces += [low * cos + high * sin, high * cos - low * sin]
            pieces.append(whole_grad[at + ROT : at + HD])
    pieces.append(whole_grad[2 * part :])
    result = jnp.concatenate(pieces, axis=0).astype(BF)
    for b in range(LEN // block):
        d_joined[b] = result[:, b * block : (b + 1) * block]


def gelu_both(hidden_in):
    normal_cdf = 0.5 * (1.0 + lax.erf(hidden_in * (1.0 / math.sqrt(2.0))))
    density = jnp.exp(-0.5 * hidden_in * hidden_in) * (1.0 / math.sqrt(2.0 * math.pi))
    return hidden_in * normal_cdf, normal_cdf + hidden_in * density


def widen_kernel(at, x, mat, bias, hidden, slope, turned):
    @pl.when(pl.program_id(0) == 0)
    def _():
        turned[...] = mat[:, at:].T

    hidden_in = jnp.dot(turned[...], x[0], preferred_element_type=F32) + column(bias[...])
    value, rise = gelu_both(hidden_in)
    hidden[0] = value.astype(BF)
    slope[0] = rise.astype(BF)


def branch_kernel(mixed, hidden, mat, out):
    cut = mixed.shape[1]
    out[0] = (
        jnp.dot(mat[:, :cut], mixed[0], preferred_element_type=F32)
        + jnp.dot(mat[:, cut:], hidden[0], preferred_element_type=F32)
    ).astype(BF)


def narrow_kernel(grad, mat, slope, d_mixed, d_hidden, turned):
    @pl.when(pl.program_id(0) == 0)
    def _():
        turned[...] = mat[...].T

    cut = d_mixed.shape[1]
    both = jnp.dot(turned[...], grad[0], preferred_element_type=F32)
    d_mixed[0] = both[:cut].astype(BF)
    d_hidden[0] = (both[cut:] * slope[0].astype(F32)).astype(BF)


def shaped_kernel(d_joined, d_hidden, qkv_mat, up_mat, out):
    cut = d_joined.shape[1]
    up_at = up_mat.shape[1] - d_hidden.shape[1]
    out[0] = (
        jnp.dot(qkv_mat[:, :cut], d_joined[0], preferred_element_type=F32)
        + jnp.dot(up_mat[:, up_at:], d_hidden[0], preferred_element_type=F32)
    ).astype(BF)


def lanes(ref):
    return jnp.concatenate([ref[b] for b in range(ref.shape[0])], axis=1)


def out_grad_kernel(grad, mixed, hidden, out):
    cut = mixed.shape[1]
    chunks, rows = out.shape[0], out.shape[1]
    left = lanes(grad)
    for item, lo in ((mixed, 0), (hidden, cut)):
        got = lax.dot_general(left, lanes(item), NT, preferred_element_type=F32).astype(BF)
        out[:, :, lo : lo + item.shape[1]] = got.reshape(chunks, rows, item.shape[1])


def in_grad_kernel(normed, grad, d_joined, d_hidden, out):
    cut = d_joined.shape[1]
    chunks, rows = out.shape[0], out.shape[1] - EXTRA
    left = lanes(normed)
    ones = jnp.ones((16, left.shape[1]), BF)
    for item, lo in ((d_joined, 0), (d_hidden, cut)):
        right = lanes(item)
        width = right.shape[0]
        got = lax.dot_general(left, right, NT, preferred_element_type=F32).astype(BF)
        sums = lax.dot_general(ones, right, NT, preferred_element_type=F32)[:8]
        out[:, :rows, lo : lo + width] = got.reshape(chunks, rows, width)
        for c in range(chunks):
            out[c, rows : rows + 8, lo : lo + width] = sums.astype(BF)
    low = lanes(grad)
    sums = lax.dot_general(ones, low, NT, preferred_element_type=F32)[:8]
    rest = out.shape[2] - sums.shape[1]
    sums = jnp.concatenate([sums, jnp.zeros((8, rest), F32)], axis=1).astype(BF)
    for c in range(chunks):
        out[c, rows + 8 :, :] = sums


def normalize(resid):
    centered = resid - jnp.mean(resid, axis=-2, keepdims=True)
    factor = lax.rsqrt(jnp.mean(centered * centered, axis=-2, keepdims=True) + 1e-05)
    return (centered * factor, factor)


def by_head(mat):
    lead, cols = mat.shape[:-1], mat.shape[-1]
    mat = mat.reshape(lead + (3, cols // (3 * HD), HD))
    return jnp.swapaxes(mat, -3, -2).reshape(lead + (cols,))


def by_kind(mat):
    lead, cols = mat.shape[:-1], mat.shape[-1]
    mat = mat.reshape(lead + (cols // (3 * HD), 3, HD))
    return jnp.swapaxes(mat, -3, -2).reshape(lead + (cols,))


def per_device(
    tokens, cotangent, ln_gain, ln_bias, w_qkv, b_qkv, w_dense, b_dense, w_fc1, b_fc1, w_fc2, b_fc2
):
    token_count, model = tokens.shape
    rows = w_qkv.shape[1]
    qkv_cols, ff_cols = w_qkv.shape[2], w_fc1.shape[2]
    mix_cols = qkv_cols // 3
    in_cols, out_cols = qkv_cols + ff_cols, mix_cols + ff_cols
    blocks = lax.axis_size("tensor")
    block = token_count // blocks
    seqs, seq_blocks = token_count // LEN, LEN // block
    ring = Ring()
    count, me = ring.count, ring.me
    tables = rotate_tables()
    gains, shifts = ln_gain.astype(F32), ln_bias.astype(F32)

    small = 4 * qkv_cols
    own = jnp.concatenate(
        [
            by_kind(
                lax.dynamic_update_slice(
                    jnp.zeros((LAYERS, qkv_cols), F32),
                    b_qkv.astype(F32),
                    (0, me * b_qkv.shape[1]),
                )
            ),
            lax.dynamic_update_slice(
                jnp.zeros((LAYERS, ff_cols), F32), b_fc1.astype(F32), (0, me * b_fc1.shape[1])
            ),
            lax.dynamic_update_slice(
                jnp.zeros((LAYERS, small - in_cols), F32),
                b_dense.astype(F32) + b_fc2.astype(F32),
                (0, me * b_dense.shape[1]),
            ),
        ],
        axis=1,
    )
    norms = jnp.concatenate([gains.reshape(4, rows), shifts.reshape(4, rows)], axis=0)
    packed = call(
        pack_kernel,
        [
            shape((rows + EXTRA, qkv_cols)),
            shape((rows, ff_cols)),
            shape((rows, out_cols)),
            shape((rows, in_cols)),
            shape((rows, out_cols)),
        ],
        moved=8 * rows * (in_cols + out_cols),
    )(norms, own, w_qkv, w_fc1, w_dense, w_fc2)
    (qkv_0, tail), gate = ring.gather(packed[0], rows)
    (up_0,), gate = ring.gather(packed[1], rows, gate)
    (out_0,), gate = ring.gather(packed[2], rows, gate)
    (in_1,), gate = ring.gather(packed[3], rows, gate)
    (out_1,), gate = ring.gather(packed[4], rows, gate)
    mats = [(qkv_0, up_0, out_0), (in_1, in_1, out_1)]
    tail = tail.reshape(LAYERS, 2, small)
    biases = tail[:, 0] + tail[:, 1]

    def turn(item):
        return jnp.swapaxes(item.reshape(blocks, block, item.shape[1]), 1, 2)

    def unturn(item):
        return jnp.swapaxes(item, 1, 2).reshape(token_count, model)

    def per_block(features):
        return pl.BlockSpec((1, features, block), lambda i: (i, 0, 0))

    def per_seq(features):
        return pl.BlockSpec((seq_blocks, features, block), lambda i: (i, 0, 0))

    def seq_lanes(features):
        return pl.BlockSpec((features, LEN), lambda i: (0, i))

    half_rot = ROT // 2
    token_blocks = turn(tokens).astype(F32)
    resid = tensor_own(token_blocks)
    stored = []
    for layer in range(LAYERS):
        qkv_mat, up_mat, out_mat = mats[layer]
        own_normed, factor = normalize(resid)
        if layer == 0:
            normed = normalize(token_blocks)[0].astype(BF)
        else:
            normed = tensor_gather(own_normed.astype(BF))
        qkv, mixed, log_total = call(
            attend_kernel,
            [
                shape((qkv_cols, token_count)),
                shape((blocks, mix_cols, block)),
                shape((8, token_count), F32),
            ],
            grid=(seqs,),
            flops=2 * token_count * (model * qkv_cols + 2 * LEN * mix_cols),
            moved=2 * model * (token_count + qkv_cols),
            in_specs=[
                per_seq(model),
                whole(qkv_mat.shape),
                whole((1, qkv_cols)),
                whole((half_rot, LEN)),
                whole((half_rot, LEN)),
            ],
            out_specs=[seq_lanes(qkv_cols), per_seq(mix_cols), seq_lanes(8)],
            scratch_shapes=[pltpu.VMEM((qkv_cols, model), BF)],
        )(normed, qkv_mat, biases[layer : layer + 1, :qkv_cols], *tables)
        hidden, slope = call(
            functools.partial(widen_kernel, up_mat.shape[1] - ff_cols),
            [shape((blocks, ff_cols, block))] * 2,
            grid=(blocks,),
            flops=2 * token_count * model * ff_cols,
            moved=2 * model * (token_count + ff_cols) + 4 * token_count * ff_cols,
            in_specs=[per_block(model), whole(up_mat.shape), whole((1, ff_cols))],
            out_specs=[per_block(ff_cols)] * 2,
            scratch_shapes=[pltpu.VMEM((ff_cols, model), BF)],
        )(normed, up_mat, biases[layer : layer + 1, qkv_cols:in_cols])
        partial = call(
            branch_kernel,
            shape((blocks, model, block)),
            grid=(blocks,),
            flops=2 * token_count * model * out_cols,
            moved=2 * model * (token_count + out_cols) + 2 * token_count * out_cols,
            in_specs=[per_block(mix_cols), per_block(ff_cols), whole(out_mat.shape)],
            out_specs=per_block(model),
        )(mixed, hidden, out_mat)
        branch = tensor_scatter(partial) + biases[layer, in_cols : in_cols + model][:, None]
        stored.append((normed, own_normed, factor, qkv, log_total, slope, mixed, hidden))
        resid = resid + branch
    output = tensor_gather(resid.astype(BF))

    grad_low = turn(cotangent)
    grad = tensor_own(grad_low).astype(F32)
    in_grads, out_grads = [None] * LAYERS, [None] * LAYERS
    for layer in reversed(range(LAYERS)):
        qkv_mat, up_mat, out_mat = mats[layer]
        normed, own_normed, factor, qkv, log_total, slope, mixed, hidden = stored[layer]
        d_mixed, d_hidden = call(
            narrow_kernel,
            [shape((blocks, mix_cols, block)), shape((blocks, ff_cols, block))],
            grid=(blocks,),
            flops=2 * token_count * model * out_cols,
            moved=2 * model * (token_count + out_cols) + 4 * token_count * out_cols,
            in_specs=[per_block(model), whole(out_mat.shape), per_block(ff_cols)],
            out_specs=[per_block(mix_cols), per_block(ff_cols)],
            scratch_shapes=[pltpu.VMEM((out_cols, model), BF)],
        )(grad_low, out_mat, slope)
        d_joined = call(
            attend_back_kernel,
            shape((blocks, qkv_cols, block)),
            grid=(seqs,),
            flops=10 * token_count * LEN * mix_cols,
            moved=6 * token_count * qkv_cols,
            in_specs=[
                seq_lanes(qkv_cols),
                seq_lanes(8),
                per_seq(mix_cols),
                whole((half_rot, LEN)),
                whole((half_rot, LEN)),
            ],
            out_specs=per_seq(qkv_cols),
            scratch_shapes=[pltpu.VMEM((qkv_cols, LEN), F32)],
        )(qkv, log_total, d_mixed, *tables)
        shaped = call(
            shaped_kernel,
            shape((blocks, model, block)),
            grid=(blocks,),
            flops=2 * token_count * model * in_cols,
            moved=2 * model * (token_count + in_cols) + 2 * token_count * in_cols,
            in_specs=[
                per_block(qkv_cols),
                per_block(ff_cols),
                whole(qkv_mat.shape),
                whole(up_mat.shape),
            ],
            out_specs=per_block(model),
        )(d_joined, d_hidden, qkv_mat, up_mat)
        parts = 2
        d_out = call(
            out_grad_kernel,
            shape((count, rows, out_cols)),
            grid=(parts,),
            flops=2 * token_count * model * out_cols,
            moved=2 * model * (token_count + out_cols) + 2 * token_count * out_cols,
            in_specs=[
                pl.BlockSpec((blocks, model // parts, block), lambda i: (0, i, 0)),
                whole((blocks, mix_cols, block)),
                whole((blocks, ff_cols, block)),
            ],
            out_specs=pl.BlockSpec((count // parts, rows, out_cols), lambda i: (i, 0, 0)),
        )(grad_low, mixed, hidden)
        out_grads[layer] = ring.scatter(d_out)
        d_in = call(
            in_grad_kernel,
            shape((count, rows + EXTRA, in_cols)),
            grid=(parts,),
            flops=2 * token_count * model * in_cols,
            moved=2 * model * (token_count + in_cols) + 2 * token_count * in_cols,
            in_specs=[
                pl.BlockSpec((blocks, model // parts, block), lambda i: (0, i, 0)),
                whole((blocks, model, block)),
                whole((blocks, qkv_cols, block)),
                whole((blocks, ff_cols, block)),
            ],
            out_specs=pl.BlockSpec((count // parts, rows + EXTRA, in_cols), lambda i: (i, 0, 0)),
        )(normed, grad_low, d_joined, d_hidden)
        in_grads[layer] = ring.scatter(d_in)
        shaped = tensor_scatter(shaped)
        grad = grad + factor * (
            shaped
            - jnp.mean(shaped, axis=0, keepdims=True)
            - own_normed * jnp.mean(shaped * own_normed, axis=0, keepdims=True)
        )
        grad_low = tensor_gather(grad.astype(BF))

    results = []
    norm_sums = []
    for layer in range(LAYERS):
        grads, sum_in = in_grads[layer][:rows], in_grads[layer][rows]
        out_sum = in_grads[layer][rows + 8]
        d_qkv = by_head(grads[:, :qkv_cols])
        sum_qkv = by_head(sum_in[:qkv_cols])
        pairs = (
            (w_qkv[layer].astype(F32), d_qkv, sum_qkv),
            (w_fc1[layer].astype(F32), grads[:, qkv_cols:], sum_in[qkv_cols:]),
        )
        norm_sums.append(
            [jnp.sum(raw * got, axis=1) for raw, got, _ in pairs]
            + [jnp.sum(raw * total[None, :], axis=1) for raw, _, total in pairs]
        )
        d_mats = [
            gains[layer, k][:, None] * got + shifts[layer, k][:, None] * total[None, :]
            for k, (_, got, total) in enumerate(pairs)
        ]
        results.append(
            (
                d_mats[0],
                lax.dynamic_slice(sum_qkv, (me * b_qkv.shape[1],), (b_qkv.shape[1],)),
                out_grads[layer][:, :mix_cols].T,
                lax.dynamic_slice(out_sum, (me * b_dense.shape[1],), (b_dense.shape[1],)),
                d_mats[1],
                lax.dynamic_slice(
                    sum_in, (qkv_cols + me * b_fc1.shape[1],), (b_fc1.shape[1],)
                ),
                out_grads[layer][:, mix_cols:].T,
            )
        )
    norm_sums = tensor_small_sum(jnp.stack([jnp.stack(item) for item in norm_sums]))

    def stacked(index):
        return jnp.stack([results[layer][index] for layer in range(LAYERS)])

    return (
        unturn(output),
        unturn(grad_low),
        norm_sums[:, :2],
        norm_sums[:, 2:],
        stacked(0),
        stacked(1),
        stacked(2),
        stacked(3),
        stacked(4),
        stacked(5),
        stacked(6),
        stacked(3),
    )


def solution(mesh):
    in_specs = (
        P("shard", None),
        P("shard", None),
        P(None, None, "shard"),
        P(None, None, "shard"),
        P(None, "shard", "tensor"),
        P(None, ("tensor", "shard")),
        P(None, "tensor", "shard"),
        P(None, "shard"),
        P(None, "shard", "tensor"),
        P(None, ("tensor", "shard")),
        P(None, "tensor", "shard"),
        P(None, "shard"),
    )
    out_specs = (
        P("shard", None),
        P("shard", None),
        P(None, None, "shard"),
        P(None, None, "shard"),
        P(None, "shard", "tensor"),
        P(None, ("tensor", "shard")),
        P(None, "tensor", "shard"),
        P(None, "shard"),
        P(None, "shard", "tensor"),
        P(None, ("tensor", "shard")),
        P(None, "tensor", "shard"),
        P(None, "shard"),
    )
    return jax.shard_map(
        per_device, mesh=mesh, in_specs=in_specs, out_specs=out_specs, check_vma=False
    )
```

```python
import functools
import math

import jax
import jax.numpy as jnp
from jax import lax
from jax.experimental import pallas as pl
from jax.experimental.pallas import tpu as pltpu
from jax.sharding import PartitionSpec as P

HD = 64
ROT = 16
LAYERS = 2
LEN = 512
EXTRA = 16
BF = jnp.bfloat16
F32 = jnp.float32
NT = (((1,), (1,)), ((), ()))
TN = (((0,), (0,)), ((), ()))
VMEM_LIMIT = 56 * 1024 * 1024


def shape(dims, dtype=BF):
    return jax.ShapeDtypeStruct(dims, dtype)


def whole(dims):
    return pl.BlockSpec(dims, lambda *_: (0,) * len(dims))


def call(kernel, out_shape, grid=None, flops=0, moved=0, **kw):
    params = pltpu.CompilerParams(vmem_limit_bytes=VMEM_LIMIT)
    cost = pl.CostEstimate(flops=int(flops), bytes_accessed=int(moved), transcendentals=0)
    if grid is not None:
        kw["grid"] = grid
    return pl.pallas_call(
        kernel, out_shape=out_shape, compiler_params=params, cost_estimate=cost, **kw
    )


def ring_order(count):
    return list(range(0, count, 2)) + list(range(count - 1, 0, -2))


def ring_perms(count):
    order = ring_order(count)
    ahead = [(order[i], order[(i + 1) % count]) for i in range(count)]
    return ahead, [(b, a) for a, b in ahead]


def after(value, *others):
    return lax.optimization_barrier((value,) + others)[0]


def assemble_kernel(count, rows, owner, *refs):
    pieces, out, rest = refs[: count + 1], refs[count + 1], refs[count + 2 :]
    half = out.shape[2] // 2
    far = count // 2
    for step in range(count):
        if step == far:
            continue
        piece = pieces[step if step < far else step + 1]
        out[owner[step]] = piece[:rows]
    out[owner[far], :, :half] = pieces[far][:rows]
    out[owner[far], :, half:] = pieces[far + 1][:rows]
    if rest:
        tail = pieces[0][rows:].astype(F32)
        for step in range(1, count):
            if step != far:
                tail = tail + pieces[step if step < far else step + 1][rows:].astype(F32)
        other = jnp.concatenate([pieces[far][rows:], pieces[far + 1][rows:]], axis=1)
        rest[0][...] = tail + other.astype(F32)


def add_first_kernel(_, left, right, up_piece, down_piece, up, down):
    half = left.shape[1]
    up[:, :half] = (up_piece[0, :, :half].astype(F32) + left[...].astype(F32)).astype(BF)
    up[:, half:] = up_piece[0, :, half:]
    down[:, :half] = down_piece[0, :, :half]
    down[:, half:] = (down_piece[0, :, half:].astype(F32) + right[...].astype(F32)).astype(BF)


def add_kernel(_, up_in, down_in, up_piece, down_piece, up, down):
    up[...] = (up_piece[0].astype(F32) + up_in[...].astype(F32)).astype(BF)
    down[...] = (down_piece[0].astype(F32) + down_in[...].astype(F32)).astype(BF)


def add_last_kernel(_, up_in, down_in, piece, out):
    out[...] = piece[0].astype(F32) + (up_in[...].astype(F32) + down_in[...].astype(F32))


class Ring:
    def __init__(self):
        self.count = lax.axis_size("shard")
        self.order = ring_order(self.count)
        self.ahead, self.back = ring_perms(self.count)
        table = [0] * self.count
        for place, device in enumerate(self.order):
            table[device] = place
        me = lax.axis_index("shard")
        place = jnp.array(table, jnp.int32)[me]
        steps = jnp.arange(self.count, dtype=jnp.int32)
        self.owner = jnp.array(self.order, jnp.int32)[(place + steps) % self.count]
        self.me = me

    def gather(self, part, rows, gate=None):
        count, cols = self.count, part.shape[1]
        half, far = cols // 2, self.count // 2
        if gate is not None:
            part = after(part, gate)
        up = down = part
        pieces = [part] + [None] * count
        for step in range(1, far):
            up = lax.ppermute(up, "shard", self.ahead)
            down = lax.ppermute(down, "shard", self.back)
            pieces[count + 1 - step] = up
            pieces[step] = down
        gate = (up, down)
        pieces[far] = lax.ppermute(up[:, :half], "shard", self.ahead)
        pieces[far + 1] = lax.ppermute(down[:, half:], "shard", self.back)
        outs = [shape((count, rows, cols))]
        if part.shape[0] > rows:
            outs.append(shape((part.shape[0] - rows, cols), F32))
        result = call(
            functools.partial(assemble_kernel, count, rows),
            outs,
            moved=4 * count * rows * cols,
            in_specs=[pl.BlockSpec(memory_space=pltpu.SMEM)]
            + [pl.BlockSpec(memory_space=pltpu.VMEM)] * (count + 1),
        )(self.owner, *pieces)
        return [result[0].reshape(count * rows, cols)] + list(result[1:]), gate

    def scatter(self, total):
        count, rows, cols = total.shape
        half, far = cols // 2, count // 2

        def add(kernel, ups, chosen, outs):
            def place(which):
                return pl.BlockSpec((1, rows, cols), lambda i, own: (own[which], 0, 0))

            return pl.pallas_call(
                kernel,
                out_shape=outs,
                grid_spec=pltpu.PrefetchScalarGridSpec(
                    num_scalar_prefetch=1,
                    grid=(1,),
                    in_specs=[whole(item.shape) for item in ups] + [place(c) for c in chosen],
                    out_specs=[whole(item.shape) for item in outs],
                ),
                compiler_params=pltpu.CompilerParams(vmem_limit_bytes=VMEM_LIMIT),
                cost_estimate=pl.CostEstimate(
                    flops=0, bytes_accessed=12 * rows * cols, transcendentals=0
                ),
            )(self.owner, *ups, *([total] * len(chosen)))

        head = lax.dynamic_index_in_dim(total, self.owner[far], 0, False)
        left = lax.ppermute(head[:, :half], "shard", self.ahead)
        right = lax.ppermute(head[:, half:], "shard", self.back)
        pair = [shape((rows, cols))] * 2
        up, down = add(add_first_kernel, (left, right), (far - 1, far + 1), pair)
        for step in range(far - 1, 0, -1):
            up = lax.ppermute(up, "shard", self.ahead)
            down = lax.ppermute(down, "shard", self.back)
            if step > 1:
                up, down = add(add_kernel, (up, down), (step - 1, count - step + 1), pair)
        return add(add_last_kernel, (up, down), (0,), [shape((rows, cols), F32)])[0]


def partner(bit):
    count = lax.axis_size("tensor")
    return [(i, i ^ (1 << bit)) for i in range(count)]


def tensor_bits():
    return lax.axis_size("tensor").bit_length() - 1


def tensor_scatter(part):
    me = lax.axis_index("tensor")
    first = None
    for bit in range(tensor_bits()):
        rows = part.shape[0] // 2
        side = (me >> bit) & 1
        keep = lax.dynamic_slice_in_dim(part, side * rows, rows, 0)
        give = lax.dynamic_slice_in_dim(part, (1 - side) * rows, rows, 0)
        got = lax.ppermute(give.astype(BF), "tensor", partner(bit))
        first = got if first is None else first
        part = keep.astype(F32) + got.astype(F32)
    return part[0], first


def tensor_own(part):
    me = lax.axis_index("tensor")
    for bit in range(tensor_bits()):
        rows = part.shape[0] // 2
        part = lax.dynamic_slice_in_dim(part, ((me >> bit) & 1) * rows, rows, 0)
    return part[0]


def tensor_gather(part):
    me = lax.axis_index("tensor")
    part = part[None]
    for bit in reversed(range(tensor_bits())):
        got = lax.ppermute(part, "tensor", partner(bit))
        side = (me >> bit) & 1
        part = jnp.where(
            side == 0, jnp.concatenate([part, got], axis=0), jnp.concatenate([got, part], axis=0)
        )
    return part


def tensor_small_sum(value):
    count = lax.axis_size("tensor")
    total = value
    for step in range(1, count):
        total = total + lax.ppermute(value, "tensor", [(i, i ^ step) for i in range(count)])
    return total


def rotate_tables():
    half = ROT // 2
    places = jnp.arange(LEN).astype(F32)
    freqs = jnp.exp(-(2.0 * jnp.arange(half).astype(F32) / ROT) * math.log(10000.0))
    angles = freqs[:, None] * places[None, :]
    return jnp.cos(angles), jnp.sin(angles)


def column(row):
    return jnp.transpose(jnp.broadcast_to(row, (8, row.shape[1])))[:, :1]


def pack_kernel(norms, own, w_qkv, w_up, w_dense, w_down, *outs):
    heads = w_qkv.shape[2] // (3 * HD)
    qkv_cols, up_cols = w_qkv.shape[2], w_up.shape[2]
    mix_cols = qkv_cols // 3
    rows = w_qkv.shape[1]
    tail = []
    for layer in range(LAYERS):
        raw = w_qkv[layer]
        by_kind = jnp.concatenate(
            [
                raw[:, (h * 3 + kind) * HD : (h * 3 + kind + 1) * HD]
                for kind in range(3)
                for h in range(heads)
            ],
            axis=1,
        )
        up = w_up[layer]
        gains = [column(norms[2 * layer + k : 2 * layer + k + 1, :]) for k in range(2)]
        shifts = [norms[4 + 2 * layer + k : 5 + 2 * layer + k, :] for k in range(2)]
        scaled = [
            (mat.astype(F32) * gain).astype(BF) for mat, gain in zip((by_kind, up), gains)
        ]
        moved = [
            jnp.dot(
                jnp.broadcast_to(row, (16, rows)).astype(BF), mat, preferred_element_type=F32
            )[:1]
            for mat, row in zip((by_kind, up), shifts)
        ]
        total = own[layer : layer + 1, :]
        pad = total.shape[1] - qkv_cols - up_cols
        total = total + jnp.concatenate(moved + [jnp.zeros((1, pad), F32)], axis=1)
        high = total.astype(BF).astype(F32)
        for value in (high, total - high):
            for at in range(0, total.shape[1], qkv_cols):
                tail.append(value[:, at : at + qkv_cols])
        first, second, at = (outs[0], outs[1], 0) if layer == 0 else (outs[2], outs[2], qkv_cols)
        first[:rows, :qkv_cols] = scaled[0]
        second[:, at : at + up_cols] = scaled[1]
        at += up_cols
        second[:, at : at + mix_cols] = w_dense[layer].astype(F32).T.astype(BF)
        second[:, at + mix_cols :] = w_down[layer].astype(F32).T.astype(BF)
    outs[0][rows:, :] = jnp.concatenate(tail, axis=0).astype(BF)


def attend_kernel(x, mat, bias, cosine, sine, qkv, mixed, log_total, turned):
    @pl.when(pl.program_id(0) == 0)
    def _():
        turned[...] = mat[:, : turned.shape[0]].T

    seq = jnp.concatenate([x[b] for b in range(x.shape[0])], axis=1)
    joined = jnp.dot(turned[...], seq, preferred_element_type=F32) + column(bias[...])
    part = joined.shape[0] // 3
    heads = part // HD
    half = ROT // 2
    cos, sin = cosine[...], sine[...]
    for kind in range(2):
        for h in range(heads):
            at = kind * part + h * HD
            low, high = joined[at : at + half], joined[at + half : at + ROT]
            turn = jnp.concatenate([low * cos - high * sin, high * cos + low * sin], axis=0)
            qkv[at : at + ROT, :] = turn.astype(BF)
            qkv[at + ROT : at + HD, :] = joined[at + ROT : at + HD].astype(BF)
    qkv[2 * part :, :] = joined[2 * part :].astype(BF)
    wide = LEN // 2
    log_total[...] = jnp.zeros_like(log_total)
    for h in range(heads):
        for q_at in range(0, LEN, wide):
            keys = q_at + wide
            query = qkv[h * HD : (h + 1) * HD, q_at:keys]
            key = qkv[part + h * HD : part + (h + 1) * HD, :keys]
            value = qkv[2 * part + h * HD : 2 * part + (h + 1) * HD, :keys]
            scores = masked_scores(key, query, q_at)
            highest = jnp.max(scores, axis=0, keepdims=True)
            chances = jnp.exp(scores - highest)
            total = jnp.sum(chances, axis=0, keepdims=True)
            out = jnp.dot(value, chances.astype(BF), preferred_element_type=F32)
            for b in range(wide // mixed.shape[2]):
                cut = slice(b * mixed.shape[2], (b + 1) * mixed.shape[2])
                at = q_at // mixed.shape[2] + b
                mixed[at, h * HD : (h + 1) * HD, :] = (out / total)[:, cut].astype(BF)
            log_total[h : h + 1, q_at:keys] = highest + jnp.log(total)


def masked_scores(key, query, q_at):
    scores = lax.dot_general(key, query, TN, preferred_element_type=F32) * (1.0 / math.sqrt(HD))
    key_at = lax.broadcasted_iota(jnp.int32, scores.shape, 0)
    query_at = lax.broadcasted_iota(jnp.int32, scores.shape, 1) + q_at
    return jnp.where(query_at >= key_at, scores, -1e30)


def attend_back_kernel(qkv, log_total, d_mixed, cosine, sine, d_joined, grads):
    part = qkv.shape[0] // 3
    heads = part // HD
    half = ROT // 2
    wide = LEN // 2
    block = d_mixed.shape[2]
    scale = 1.0 / math.sqrt(HD)
    cos, sin = cosine[...], sine[...]
    for h in range(heads):
        d_key, d_value = [], []
        for q_at in range(0, LEN, wide):
            keys = q_at + wide
            query = qkv[h * HD : (h + 1) * HD, q_at:keys]
            key = qkv[part + h * HD : part + (h + 1) * HD, :keys]
            value = qkv[2 * part + h * HD : 2 * part + (h + 1) * HD, :keys]
            d_out = jnp.concatenate(
                [
                    d_mixed[q_at // block + b, h * HD : (h + 1) * HD, :]
                    for b in range(wide // block)
                ],
                axis=1,
            )
            scores = masked_scores(key, query, q_at)
            chances = jnp.exp(scores - log_total[h : h + 1, q_at:keys])
            d_chances = lax.dot_general(value, d_out, TN, preferred_element_type=F32)
            weighted = chances * d_chances
            inner = jnp.sum(weighted, axis=0, keepdims=True)
            d_scores = (weighted - chances * inner).astype(BF)
            grads[h * HD : (h + 1) * HD, q_at:keys] = (
                jnp.dot(key, d_scores, preferred_element_type=F32) * scale
            )
            d_key.append(lax.dot_general(query, d_scores, NT, preferred_element_type=F32))
            d_value.append(
                lax.dot_general(d_out, chances.astype(BF), NT, preferred_element_type=F32)
            )
        for base, items, factor in ((part, d_key, scale), (2 * part, d_value, 1.0)):
            at = base + h * HD
            grads[at : at + HD, :wide] = (items[0] + items[1][:, :wide]) * factor
            grads[at : at + HD, wide:] = items[1][:, wide:] * factor
    whole_grad = grads[...]
    pieces = []
    for kind in range(2):
        for h in range(heads):
            at = kind * part + h * HD
            low, high = whole_grad[at : at + half], whole_grad[at + half : at + ROT]
            pieces += [low * cos + high * sin, high * cos - low * sin]
            pieces.append(whole_grad[at + ROT : at + HD])
    pieces.append(whole_grad[2 * part :])
    result = jnp.concatenate(pieces, axis=0).astype(BF)
    for b in range(LEN // block):
        d_joined[b] = result[:, b * block : (b + 1) * block]


def gelu_both(hidden_in):
    normal_cdf = 0.5 * (1.0 + lax.erf(hidden_in * (1.0 / math.sqrt(2.0))))
    density = jnp.exp(-0.5 * hidden_in * hidden_in) * (1.0 / math.sqrt(2.0 * math.pi))
    return hidden_in * normal_cdf, normal_cdf + hidden_in * density


def widen_kernel(at, x, mat, bias, hidden, slope, turned):
    @pl.when(pl.program_id(0) == 0)
    def _():
        turned[...] = mat[:, at : at + turned.shape[0]].T

    hidden_in = jnp.dot(turned[...], x[0], preferred_element_type=F32) + column(bias[...])
    value, rise = gelu_both(hidden_in)
    hidden[0] = value.astype(BF)
    slope[0] = rise.astype(BF)


def branch_kernel(at, mixed, hidden, mat, out):
    cut = at + mixed.shape[1]
    out[0] = (
        jnp.dot(mat[:, at:cut], mixed[0], preferred_element_type=F32)
        + jnp.dot(mat[:, cut:], hidden[0], preferred_element_type=F32)
    ).astype(BF)


def narrow_kernel(at, grad, mat, slope, d_mixed, d_hidden, turned):
    @pl.when(pl.program_id(0) == 0)
    def _():
        turned[...] = mat[:, at:].T

    cut = d_mixed.shape[1]
    both = jnp.dot(turned[...], grad[0], preferred_element_type=F32)
    d_mixed[0] = both[:cut].astype(BF)
    d_hidden[0] = (both[cut:] * slope[0].astype(F32)).astype(BF)


def shaped_kernel(at, d_joined, d_hidden, qkv_mat, up_mat, out):
    cut, end = d_joined.shape[1], at + d_hidden.shape[1]
    out[0] = (
        jnp.dot(qkv_mat[:, :cut], d_joined[0], preferred_element_type=F32)
        + jnp.dot(up_mat[:, at:end], d_hidden[0], preferred_element_type=F32)
    ).astype(BF)


def lanes(ref):
    return jnp.concatenate([ref[b] for b in range(ref.shape[0])], axis=1)


def grad_kernel(pairs, sums, *refs):
    ins, out = refs[:-1], refs[-1]
    chunks = out.shape[0]
    rows = out.shape[1] - (EXTRA if sums else 0)
    lo = 0
    for left, right in pairs:
        width = ins[right].shape[1]
        got = lax.dot_general(
            lanes(ins[left]), lanes(ins[right]), NT, preferred_element_type=F32
        ).astype(BF)
        out[:, :rows, lo : lo + width] = got.reshape(chunks, rows, width)
        lo += width
    if sums:
        total = []
        for item in sums:
            right = lanes(ins[item])
            ones = jnp.ones((16, right.shape[1]), BF)
            total.append(lax.dot_general(ones, right, NT, preferred_element_type=F32)[:1])
        qkv_cols = ins[sums[0]].shape[1]
        used = sum(item.shape[1] for item in total)
        total = jnp.concatenate(total + [jnp.zeros((1, 4 * qkv_cols - used), F32)], axis=1)
        tail = [total[:, at : at + qkv_cols] for at in range(0, 4 * qkv_cols, qkv_cols)]
        tail = jnp.concatenate(tail + [jnp.zeros((EXTRA - 4, qkv_cols), F32)], axis=0).astype(BF)
        for c in range(chunks):
            out[c, rows:, :qkv_cols] = tail
            if out.shape[2] > qkv_cols:
                out[c, rows:, qkv_cols:] = jnp.zeros((EXTRA, out.shape[2] - qkv_cols), BF)


def finish_kernel(layer, split, norms, w_qkv, w_up, *refs):
    parts, outs = refs[: 1 + split], refs[-6:]
    d_qkv, d_up, d_dense, d_down, d_norm, sums = outs
    rows, qkv_cols = w_qkv.shape[1], w_qkv.shape[2]
    up_cols, mix_cols = w_up.shape[2], d_dense.shape[1]
    heads = qkv_cols // (3 * HD)
    got = parts[0][:rows, :qkv_cols].astype(F32)
    tail = parts[0][rows:, :qkv_cols].astype(F32)
    rest = parts[1][...] if split else parts[0][:rows, qkv_cols:].astype(F32)
    total = jnp.concatenate([tail[r : r + 1] for r in range(4)], axis=1)
    sums[0] = total
    gains = [column(norms[2 * layer + k : 2 * layer + k + 1, :]) for k in range(2)]
    shifts = [column(norms[4 + 2 * layer + k : 5 + 2 * layer + k, :]) for k in range(2)]
    raw = w_qkv[0].astype(F32)
    full = gains[0] * got + shifts[0] * total[:, :qkv_cols]
    gain_sum = jnp.zeros((rows, 1), F32)
    shift_sum = jnp.zeros((rows, 1), F32)
    for h in range(heads):
        for kind in range(3):
            to, at = (h * 3 + kind) * HD, (kind * heads + h) * HD
            d_qkv[0, :, to : to + HD] = full[:, at : at + HD]
            piece = raw[:, to : to + HD]
            gain_sum += jnp.sum(piece * got[:, at : at + HD], axis=1, keepdims=True)
            shift_sum += jnp.sum(piece * total[:, at : at + HD], axis=1, keepdims=True)
    up_sum = total[:, qkv_cols : qkv_cols + up_cols]
    raw = w_up[0].astype(F32)
    d_up[0] = gains[1] * rest[:, :up_cols] + shifts[1] * up_sum
    columns = [
        gain_sum,
        jnp.sum(raw * rest[:, :up_cols], axis=1, keepdims=True),
        shift_sum,
        jnp.sum(raw * up_sum, axis=1, keepdims=True),
        jnp.zeros((rows, 4), F32),
    ]
    d_norm[0] = jnp.transpose(jnp.concatenate(columns, axis=1))
    d_dense[0] = jnp.transpose(rest[:, up_cols : up_cols + mix_cols])
    d_down[0] = jnp.transpose(rest[:, up_cols + mix_cols :])


def normalize(resid):
    centered = resid - jnp.mean(resid, axis=-2, keepdims=True)
    factor = lax.rsqrt(jnp.mean(centered * centered, axis=-2, keepdims=True) + 1e-05)
    return (centered * factor, factor)


def by_head(mat):
    lead, cols = mat.shape[:-1], mat.shape[-1]
    mat = mat.reshape(lead + (3, cols // (3 * HD), HD))
    return jnp.swapaxes(mat, -3, -2).reshape(lead + (cols,))


def by_kind(mat):
    lead, cols = mat.shape[:-1], mat.shape[-1]
    mat = mat.reshape(lead + (cols // (3 * HD), 3, HD))
    return jnp.swapaxes(mat, -3, -2).reshape(lead + (cols,))


def per_device(
    tokens, cotangent, ln_gain, ln_bias, w_qkv, b_qkv, w_dense, b_dense, w_fc1, b_fc1, w_fc2, b_fc2
):
    token_count, model = tokens.shape
    rows = w_qkv.shape[1]
    qkv_cols, ff_cols = w_qkv.shape[2], w_fc1.shape[2]
    mix_cols = qkv_cols // 3
    in_cols, out_cols = qkv_cols + ff_cols, mix_cols + ff_cols
    blocks = lax.axis_size("tensor")
    block = token_count // blocks
    seqs, seq_blocks = token_count // LEN, LEN // block
    ring = Ring()
    count, me = ring.count, ring.me
    tables = rotate_tables()
    gains, shifts = ln_gain.astype(F32), ln_bias.astype(F32)

    small = 4 * qkv_cols
    own = jnp.concatenate(
        [
            by_kind(
                lax.dynamic_update_slice(
                    jnp.zeros((LAYERS, qkv_cols), F32),
                    b_qkv.astype(F32),
                    (0, me * b_qkv.shape[1]),
                )
            ),
            lax.dynamic_update_slice(
                jnp.zeros((LAYERS, ff_cols), F32), b_fc1.astype(F32), (0, me * b_fc1.shape[1])
            ),
            lax.dynamic_update_slice(
                jnp.zeros((LAYERS, small - in_cols), F32),
                b_dense.astype(F32) + b_fc2.astype(F32),
                (0, me * b_dense.shape[1]),
            ),
        ],
        axis=1,
    )
    norms = jnp.concatenate([gains.reshape(4, rows), shifts.reshape(4, rows)], axis=0)
    rest_cols = ff_cols + out_cols
    packed = call(
        pack_kernel,
        [
            shape((rows + EXTRA, qkv_cols)),
            shape((rows, rest_cols)),
            shape((rows, in_cols + out_cols)),
        ],
        moved=8 * rows * (in_cols + out_cols),
    )(norms, own, w_qkv, w_fc1, w_dense, w_fc2)
    (qkv_0, tail), gate = ring.gather(packed[0], rows)
    all_1 = lax.all_gather(after(packed[2], gate), "shard", axis=0, tiled=True)
    (rest_0,), gate = ring.gather(packed[1], rows, gate)
    mats = [
        ((qkv_0, 0), (rest_0, 0), (rest_0, ff_cols)),
        ((all_1, 0), (all_1, qkv_cols), (all_1, in_cols)),
    ]
    tail = tail.reshape(LAYERS, 2, small)
    biases = tail[:, 0] + tail[:, 1]

    def turn(item):
        return jnp.swapaxes(item.reshape(blocks, block, item.shape[1]), 1, 2)

    def unturn(item):
        return jnp.swapaxes(item, 1, 2).reshape(token_count, model)

    def per_block(features):
        return pl.BlockSpec((1, features, block), lambda i: (i, 0, 0))

    def per_seq(features):
        return pl.BlockSpec((seq_blocks, features, block), lambda i: (i, 0, 0))

    def seq_lanes(features):
        return pl.BlockSpec((features, LEN), lambda i: (0, i))

    half_rot = ROT // 2
    block_of = lambda features: whole((blocks, features, block))

    def attend(normed, layer):
        mat, _ = mats[layer][0]
        return call(
            attend_kernel,
            [
                shape((qkv_cols, token_count)),
                shape((blocks, mix_cols, block)),
                shape((8, token_count), F32),
            ],
            grid=(seqs,),
            flops=2 * token_count * (model * qkv_cols + 2 * LEN * mix_cols),
            moved=2 * model * (token_count + qkv_cols),
            in_specs=[
                per_seq(model),
                whole((model, qkv_cols)),
                whole((1, qkv_cols)),
                whole((half_rot, LEN)),
                whole((half_rot, LEN)),
            ],
            out_specs=[seq_lanes(qkv_cols), per_seq(mix_cols), seq_lanes(8)],
            scratch_shapes=[pltpu.VMEM((qkv_cols, model), BF)],
        )(normed, mat, biases[layer : layer + 1, :qkv_cols], *tables)

    def widen(normed, layer):
        mat, at = mats[layer][1]
        return call(
            functools.partial(widen_kernel, at),
            [shape((blocks, ff_cols, block))] * 2,
            grid=(blocks,),
            flops=2 * token_count * model * ff_cols,
            moved=2 * model * (token_count + ff_cols) + 4 * token_count * ff_cols,
            in_specs=[per_block(model), whole(mat.shape), whole((1, ff_cols))],
            out_specs=[per_block(ff_cols)] * 2,
            scratch_shapes=[pltpu.VMEM((ff_cols, model), BF)],
        )(normed, mat, biases[layer : layer + 1, qkv_cols:in_cols])

    def branch_of(mixed, hidden, layer):
        mat, at = mats[layer][2]
        return call(
            functools.partial(branch_kernel, at),
            shape((blocks, model, block)),
            grid=(blocks,),
            flops=2 * token_count * model * out_cols,
            moved=2 * model * (token_count + out_cols) + 2 * token_count * out_cols,
            in_specs=[per_block(mix_cols), per_block(ff_cols), whole(mat.shape)],
            out_specs=per_block(model),
        )(mixed, hidden, mat)

    def narrow(grad_low, slope, layer):
        mat, at = mats[layer][2]
        return call(
            functools.partial(narrow_kernel, at),
            [shape((blocks, mix_cols, block)), shape((blocks, ff_cols, block))],
            grid=(blocks,),
            flops=2 * token_count * model * out_cols,
            moved=2 * model * (token_count + out_cols) + 4 * token_count * out_cols,
            in_specs=[per_block(model), whole(mat.shape), per_block(ff_cols)],
            out_specs=[per_block(mix_cols), per_block(ff_cols)],
            scratch_shapes=[pltpu.VMEM((out_cols, model), BF)],
        )(grad_low, mat, slope)

    def attend_back(qkv, log_total, d_mixed):
        return call(
            attend_back_kernel,
            shape((blocks, qkv_cols, block)),
            grid=(seqs,),
            flops=10 * token_count * LEN * mix_cols,
            moved=6 * token_count * qkv_cols,
            in_specs=[
                seq_lanes(qkv_cols),
                seq_lanes(8),
                per_seq(mix_cols),
                whole((half_rot, LEN)),
                whole((half_rot, LEN)),
            ],
            out_specs=per_seq(qkv_cols),
            scratch_shapes=[pltpu.VMEM((qkv_cols, LEN), F32)],
        )(qkv, log_total, d_mixed, *tables)

    def shaped_of(d_joined, d_hidden, layer):
        (qkv_mat, _), (up_mat, at) = mats[layer][:2]
        return call(
            functools.partial(shaped_kernel, at),
            shape((blocks, model, block)),
            grid=(blocks,),
            flops=2 * token_count * model * in_cols,
            moved=2 * model * (token_count + in_cols) + 2 * token_count * in_cols,
            in_specs=[
                per_block(qkv_cols),
                per_block(ff_cols),
                whole((model, qkv_cols)),
                whole(up_mat.shape),
            ],
            out_specs=per_block(model),
        )(d_joined, d_hidden, qkv_mat, up_mat)

    def grads_of(pairs, sums, *items):
        parts = 2
        lefts = {left for left, _ in pairs}
        cols = sum(items[right].shape[1] for _, right in pairs)
        high = rows + (EXTRA if sums else 0)
        return call(
            functools.partial(grad_kernel, pairs, sums),
            shape((count, high, cols)),
            grid=(parts,),
            flops=2 * token_count * model * cols,
            moved=2 * model * (token_count + cols) + 2 * token_count * cols,
            in_specs=[
                pl.BlockSpec((blocks, model // parts, block), lambda i: (0, i, 0))
                if k in lefts
                else block_of(item.shape[1])
                for k, item in enumerate(items)
            ],
            out_specs=pl.BlockSpec((count // parts, high, cols), lambda i: (i, 0, 0)),
        )(*items)

    def grad_step(grad, shaped, own_normed, factor):
        return grad + factor * (
            shaped
            - jnp.mean(shaped, axis=0, keepdims=True)
            - own_normed * jnp.mean(shaped * own_normed, axis=0, keepdims=True)
        )

    token_blocks = turn(tokens).astype(F32)
    resid_0 = tensor_own(token_blocks)
    own_normed_0, factor_0 = normalize(resid_0)
    normed_0 = normalize(token_blocks)[0].astype(BF)
    qkv_rows_0, mixed_0, log_0 = attend(normed_0, 0)
    hidden_0, slope_0 = widen(normed_0, 0)
    branch, _ = tensor_scatter(branch_of(mixed_0, hidden_0, 0))
    resid_1 = resid_0 + branch + biases[0, in_cols : in_cols + model][:, None]
    own_normed_1, factor_1 = normalize(resid_1)
    normed_1 = tensor_gather(own_normed_1.astype(BF))
    qkv_rows_1, mixed_1, log_1 = attend(normed_1, 1)
    hidden_1, slope_1 = widen(normed_1, 1)

    grad_low_2 = turn(cotangent)
    d_mixed, d_hidden = narrow(grad_low_2, slope_1, 1)
    d_joined = attend_back(qkv_rows_1, log_1, d_mixed)
    shaped, met = tensor_scatter(shaped_of(d_joined, d_hidden, 1))
    total_1 = grads_of(
        ((0, 2), (0, 3), (1, 4), (1, 5)),
        (2, 3, 6),
        after(normed_1, met),
        grad_low_2,
        d_joined,
        d_hidden,
        mixed_1,
        hidden_1,
        grad_low_2,
    )
    sum_1 = lax.psum_scatter(total_1, "shard", scatter_dimension=0, tiled=True)[0]
    grad_1 = grad_step(tensor_own(grad_low_2).astype(F32), shaped, own_normed_1, factor_1)
    grad_low_1 = tensor_gather(grad_1.astype(BF))

    branch, _ = tensor_scatter(branch_of(mixed_1, after(hidden_1, total_1), 1))
    resid_2 = resid_1 + branch + biases[1, in_cols : in_cols + model][:, None]
    output = tensor_gather(resid_2.astype(BF))

    d_mixed, d_hidden = narrow(grad_low_1, slope_0, 0)
    rest_sum = ring.scatter(
        grads_of(((0, 2), (1, 3), (1, 4)), (), normed_0, grad_low_1, d_hidden, mixed_0, hidden_0)
    )
    d_joined = attend_back(qkv_rows_0, log_0, d_mixed)
    qkv_sum = ring.scatter(
        grads_of(((0, 1),), (1, 2, 3), normed_0, d_joined, d_hidden, grad_low_1)
    )
    shaped, _ = tensor_scatter(shaped_of(d_joined, d_hidden, 0))
    grad_0 = grad_step(grad_1, shaped, own_normed_0, factor_0)
    grad_low_0 = tensor_gather(grad_0.astype(BF))

    def finish(layer, parts, kept):
        def at(dims):
            return pl.BlockSpec((1,) + dims, lambda i: (layer, 0, 0))

        outs = [
            (rows, qkv_cols), (rows, ff_cols), w_dense.shape[1:], w_fc2.shape[1:], (8, rows),
            (1, small),
        ]
        first = 3 + len(parts)
        return call(
            functools.partial(finish_kernel, layer, len(parts) - 1),
            [shape((LAYERS,) + item, F32) for item in outs],
            grid=(1,),
            moved=8 * rows * (in_cols + out_cols),
            in_specs=[whole(norms.shape), at((rows, qkv_cols)), at((rows, ff_cols))]
            + [whole(item.shape) for item in parts]
            + [pl.BlockSpec(memory_space=pl.ANY)] * len(kept),
            out_specs=[at(item) for item in outs],
            input_output_aliases={first + k: k for k in range(len(kept))},
        )(norms, w_qkv, w_fc1, *parts, *kept)

    kept = finish(1, (sum_1,), ())
    d_qkv, d_up, d_dense, d_down, d_norm, sums = finish(0, (qkv_sum, rest_sum), kept)
    d_norm = tensor_small_sum(d_norm)
    sums = sums[:, 0]
    d_out_bias = lax.dynamic_slice(
        sums, (0, in_cols + me * b_dense.shape[1]), b_dense.shape
    )
    return (
        unturn(output),
        unturn(grad_low_0),
        d_norm[:, :2],
        d_norm[:, 2:4],
        d_qkv,
        lax.dynamic_slice(by_head(sums[:, :qkv_cols]), (0, me * b_qkv.shape[1]), b_qkv.shape),
        d_dense,
        d_out_bias,
        d_up,
        lax.dynamic_slice(sums, (0, qkv_cols + me * b_fc1.shape[1]), b_fc1.shape),
        d_down,
        d_out_bias,
    )


def solution(mesh):
    in_specs = (
        P("shard", None),
        P("shard", None),
        P(None, None, "shard"),
        P(None, None, "shard"),
        P(None, "shard", "tensor"),
        P(None, ("tensor", "shard")),
        P(None, "tensor", "shard"),
        P(None, "shard"),
        P(None, "shard", "tensor"),
        P(None, ("tensor", "shard")),
        P(None, "tensor", "shard"),
        P(None, "shard"),
    )
    out_specs = (
        P("shard", None),
        P("shard", None),
        P(None, None, "shard"),
        P(None, None, "shard"),
        P(None, "shard", "tensor"),
        P(None, ("tensor", "shard")),
        P(None, "tensor", "shard"),
        P(None, "shard"),
        P(None, "shard", "tensor"),
        P(None, ("tensor", "shard")),
        P(None, "tensor", "shard"),
        P(None, "shard"),
    )
    return jax.shard_map(
        per_device, mesh=mesh, in_specs=in_specs, out_specs=out_specs, check_vma=False
    )
```

```python
import functools
import math

import jax
import jax.numpy as jnp
from jax import lax
from jax.experimental import pallas as pl
from jax.experimental.pallas import tpu as pltpu
from jax.sharding import PartitionSpec as P

HD = 64
ROT = 16
LAYERS = 2
LEN = 512
EXTRA = 16
BF = jnp.bfloat16
F32 = jnp.float32
NT = (((1,), (1,)), ((), ()))
TN = (((0,), (0,)), ((), ()))
VMEM_LIMIT = 56 * 1024 * 1024


def shape(dims, dtype=BF):
    return jax.ShapeDtypeStruct(dims, dtype)


def whole(dims):
    return pl.BlockSpec(dims, lambda *_: (0,) * len(dims))


def call(kernel, out_shape, grid=None, flops=0, moved=0, **kw):
    params = pltpu.CompilerParams(vmem_limit_bytes=VMEM_LIMIT)
    cost = pl.CostEstimate(flops=int(flops), bytes_accessed=int(moved), transcendentals=0)
    if grid is not None:
        kw["grid"] = grid
    return pl.pallas_call(
        kernel, out_shape=out_shape, compiler_params=params, cost_estimate=cost, **kw
    )


def ring_order(count):
    return list(range(0, count, 2)) + list(range(count - 1, 0, -2))


def ring_perms(count):
    order = ring_order(count)
    ahead = [(order[i], order[(i + 1) % count]) for i in range(count)]
    return ahead, [(b, a) for a, b in ahead]


def after(value, *others):
    return lax.optimization_barrier((value,) + others)[0]


def assemble_kernel(count, rows, owner, *refs):
    pieces, out, rest = refs[: count + 1], refs[count + 1], refs[count + 2 :]
    half = out.shape[2] // 2
    far = count // 2
    for step in range(count):
        if step == far:
            continue
        piece = pieces[step if step < far else step + 1]
        out[owner[step]] = piece[:rows]
    out[owner[far], :, :half] = pieces[far][:rows]
    out[owner[far], :, half:] = pieces[far + 1][:rows]
    if rest:
        tail = pieces[0][rows:].astype(F32)
        for step in range(1, count):
            if step != far:
                tail = tail + pieces[step if step < far else step + 1][rows:].astype(F32)
        other = jnp.concatenate([pieces[far][rows:], pieces[far + 1][rows:]], axis=1)
        rest[0][...] = tail + other.astype(F32)


def add_first_kernel(_, left, right, up_piece, down_piece, up, down):
    half = left.shape[1]
    up[:, :half] = (up_piece[0, :, :half].astype(F32) + left[...].astype(F32)).astype(BF)
    up[:, half:] = up_piece[0, :, half:]
    down[:, :half] = down_piece[0, :, :half]
    down[:, half:] = (down_piece[0, :, half:].astype(F32) + right[...].astype(F32)).astype(BF)


def add_kernel(_, up_in, down_in, up_piece, down_piece, up, down):
    up[...] = (up_piece[0].astype(F32) + up_in[...].astype(F32)).astype(BF)
    down[...] = (down_piece[0].astype(F32) + down_in[...].astype(F32)).astype(BF)


def add_last_kernel(_, up_in, down_in, piece, out):
    out[...] = piece[0].astype(F32) + (up_in[...].astype(F32) + down_in[...].astype(F32))


class Ring:
    def __init__(self):
        self.count = lax.axis_size("shard")
        self.order = ring_order(self.count)
        self.ahead, self.back = ring_perms(self.count)
        table = [0] * self.count
        for place, device in enumerate(self.order):
            table[device] = place
        me = lax.axis_index("shard")
        place = jnp.array(table, jnp.int32)[me]
        steps = jnp.arange(self.count, dtype=jnp.int32)
        self.owner = jnp.array(self.order, jnp.int32)[(place + steps) % self.count]
        self.me = me

    def gather(self, part, rows, gate=None, holds=None):
        count, cols = self.count, part.shape[1]
        half, far = cols // 2, self.count // 2
        if gate is not None:
            part = after(part, *gate)
        up = down = part
        pieces = [part] + [None] * count
        holds = holds or {}
        gate = []
        for step in range(1, far):
            if step in holds:
                up, down = lax.optimization_barrier((up, down, holds[step]))[:2]
            up = lax.ppermute(up, "shard", self.ahead)
            down = lax.ppermute(down, "shard", self.back)
            pieces[count + 1 - step] = up
            pieces[step] = down
            gate.append((up, down))
        pieces[far] = lax.ppermute(up[:, :half], "shard", self.ahead)
        pieces[far + 1] = lax.ppermute(down[:, half:], "shard", self.back)
        outs = [shape((count, rows, cols))]
        if part.shape[0] > rows:
            outs.append(shape((part.shape[0] - rows, cols), F32))
        result = call(
            functools.partial(assemble_kernel, count, rows),
            outs,
            moved=4 * count * rows * cols,
            in_specs=[pl.BlockSpec(memory_space=pltpu.SMEM)]
            + [pl.BlockSpec(memory_space=pltpu.VMEM)] * (count + 1),
        )(self.owner, *pieces)
        return [result[0].reshape(count * rows, cols)] + list(result[1:]), gate

    def scatter(self, total, hold=None):
        count, rows, cols = total.shape
        half, far = cols // 2, count // 2

        def add(kernel, ups, chosen, outs, total=total):
            def place(which):
                return pl.BlockSpec((1, rows, cols), lambda i, own: (own[which], 0, 0))

            return pl.pallas_call(
                kernel,
                out_shape=outs,
                grid_spec=pltpu.PrefetchScalarGridSpec(
                    num_scalar_prefetch=1,
                    grid=(1,),
                    in_specs=[whole(item.shape) for item in ups] + [place(c) for c in chosen],
                    out_specs=[whole(item.shape) for item in outs],
                ),
                compiler_params=pltpu.CompilerParams(vmem_limit_bytes=VMEM_LIMIT),
                cost_estimate=pl.CostEstimate(
                    flops=0, bytes_accessed=12 * rows * cols, transcendentals=0
                ),
            )(self.owner, *ups, *([total] * len(chosen)))

        head = lax.dynamic_index_in_dim(total, self.owner[far], 0, False)
        left = lax.ppermute(head[:, :half], "shard", self.ahead)
        right = lax.ppermute(head[:, half:], "shard", self.back)
        pair = [shape((rows, cols))] * 2
        up, down = add(add_first_kernel, (left, right), (far - 1, far + 1), pair)
        for step in range(far - 1, 0, -1):
            up = lax.ppermute(up, "shard", self.ahead)
            down = lax.ppermute(down, "shard", self.back)
            if step > 1:
                up, down = add(add_kernel, (up, down), (step - 1, count - step + 1), pair)
        if hold is not None:
            total = after(total, hold)
        return add(add_last_kernel, (up, down), (0,), [shape((rows, cols), F32)], total)[0]


def partner(bit):
    count = lax.axis_size("tensor")
    return [(i, i ^ (1 << bit)) for i in range(count)]


def tensor_bits():
    return lax.axis_size("tensor").bit_length() - 1


def tensor_scatter(part):
    me = lax.axis_index("tensor")
    first = None
    for bit in range(tensor_bits()):
        rows = part.shape[0] // 2
        side = (me >> bit) & 1
        keep = lax.dynamic_slice_in_dim(part, side * rows, rows, 0)
        give = lax.dynamic_slice_in_dim(part, (1 - side) * rows, rows, 0)
        got = lax.ppermute(give.astype(BF), "tensor", partner(bit))
        first = give
        part = keep.astype(F32) + got.astype(F32)
    return part[0], first


def tensor_own(part):
    me = lax.axis_index("tensor")
    for bit in range(tensor_bits()):
        rows = part.shape[0] // 2
        part = lax.dynamic_slice_in_dim(part, ((me >> bit) & 1) * rows, rows, 0)
    return part[0]


def tensor_gather(part):
    me = lax.axis_index("tensor")
    part = part[None]
    for bit in reversed(range(tensor_bits())):
        got = lax.ppermute(part, "tensor", partner(bit))
        side = (me >> bit) & 1
        part = jnp.where(
            side == 0, jnp.concatenate([part, got], axis=0), jnp.concatenate([got, part], axis=0)
        )
    return part


def tensor_small_sum(value):
    count = lax.axis_size("tensor")
    total = value
    for step in range(1, count):
        total = total + lax.ppermute(value, "tensor", [(i, i ^ step) for i in range(count)])
    return total


def rotate_tables():
    half = ROT // 2
    places = jnp.arange(LEN).astype(F32)
    freqs = jnp.exp(-(2.0 * jnp.arange(half).astype(F32) / ROT) * math.log(10000.0))
    angles = freqs[:, None] * places[None, :]
    return jnp.cos(angles), jnp.sin(angles)


def column(row):
    return jnp.transpose(jnp.broadcast_to(row, (8, row.shape[1])))[:, :1]


def pack_kernel(norms, own, w_qkv, w_up, w_dense, w_down, *outs):
    heads = w_qkv.shape[2] // (3 * HD)
    qkv_cols, up_cols = w_qkv.shape[2], w_up.shape[2]
    mix_cols = qkv_cols // 3
    rows = w_qkv.shape[1]
    tail = []
    for layer in range(LAYERS):
        raw = w_qkv[layer]
        by_kind = jnp.concatenate(
            [
                raw[:, (h * 3 + kind) * HD : (h * 3 + kind + 1) * HD]
                for kind in range(3)
                for h in range(heads)
            ],
            axis=1,
        )
        up = w_up[layer]
        gains = [column(norms[2 * layer + k : 2 * layer + k + 1, :]) for k in range(2)]
        shifts = [norms[4 + 2 * layer + k : 5 + 2 * layer + k, :] for k in range(2)]
        scaled = [
            (mat.astype(F32) * gain).astype(BF) for mat, gain in zip((by_kind, up), gains)
        ]
        moved = [
            jnp.dot(
                jnp.broadcast_to(row, (16, rows)).astype(BF), mat, preferred_element_type=F32
            )[:1]
            for mat, row in zip((by_kind, up), shifts)
        ]
        total = own[layer : layer + 1, :]
        pad = total.shape[1] - qkv_cols - up_cols
        total = total + jnp.concatenate(moved + [jnp.zeros((1, pad), F32)], axis=1)
        high = total.astype(BF).astype(F32)
        for value in (high, total - high):
            for at in range(0, total.shape[1], qkv_cols):
                tail.append(value[:, at : at + qkv_cols])
        first, second, third = (0, 1, 1) if layer == 0 else (2, 2, 3)
        outs[first][:rows, :qkv_cols] = scaled[0]
        at = 0 if layer == 0 else qkv_cols
        outs[second][:, at : at + up_cols] = scaled[1]
        at = up_cols if layer == 0 else 0
        outs[third][:, at : at + mix_cols] = w_dense[layer].astype(F32).T.astype(BF)
        outs[third][:, at + mix_cols :] = w_down[layer].astype(F32).T.astype(BF)
    outs[0][rows:, :] = jnp.concatenate(tail, axis=0).astype(BF)


def attend_kernel(x, mat, bias, cosine, sine, qkv, mixed, log_total, turned):
    @pl.when(pl.program_id(0) == 0)
    def _():
        turned[...] = mat[:, : turned.shape[0]].T

    seq = jnp.concatenate([x[b] for b in range(x.shape[0])], axis=1)
    joined = jnp.dot(turned[...], seq, preferred_element_type=F32) + column(bias[...])
    part = joined.shape[0] // 3
    heads = part // HD
    half = ROT // 2
    cos, sin = cosine[...], sine[...]
    for kind in range(2):
        for h in range(heads):
            at = kind * part + h * HD
            low, high = joined[at : at + half], joined[at + half : at + ROT]
            turn = jnp.concatenate([low * cos - high * sin, high * cos + low * sin], axis=0)
            qkv[at : at + ROT, :] = turn.astype(BF)
            qkv[at + ROT : at + HD, :] = joined[at + ROT : at + HD].astype(BF)
    qkv[2 * part :, :] = joined[2 * part :].astype(BF)
    wide = LEN // 2
    log_total[...] = jnp.zeros_like(log_total)
    for h in range(heads):
        for q_at in range(0, LEN, wide):
            keys = q_at + wide
            query = qkv[h * HD : (h + 1) * HD, q_at:keys]
            key = qkv[part + h * HD : part + (h + 1) * HD, :keys]
            value = qkv[2 * part + h * HD : 2 * part + (h + 1) * HD, :keys]
            scores = masked_scores(key, query, q_at)
            highest = jnp.max(scores, axis=0, keepdims=True)
            chances = jnp.exp(scores - highest)
            total = jnp.sum(chances, axis=0, keepdims=True)
            out = jnp.dot(value, chances.astype(BF), preferred_element_type=F32)
            for b in range(wide // mixed.shape[2]):
                cut = slice(b * mixed.shape[2], (b + 1) * mixed.shape[2])
                at = q_at // mixed.shape[2] + b
                mixed[at, h * HD : (h + 1) * HD, :] = (out / total)[:, cut].astype(BF)
            log_total[h : h + 1, q_at:keys] = highest + jnp.log(total)


def masked_scores(key, query, q_at):
    scores = lax.dot_general(key, query, TN, preferred_element_type=F32) * (1.0 / math.sqrt(HD))
    key_at = lax.broadcasted_iota(jnp.int32, scores.shape, 0)
    query_at = lax.broadcasted_iota(jnp.int32, scores.shape, 1) + q_at
    return jnp.where(query_at >= key_at, scores, -1e30)


def attend_back_kernel(qkv, log_total, d_mixed, cosine, sine, d_joined, grads):
    part = qkv.shape[0] // 3
    heads = part // HD
    half = ROT // 2
    wide = LEN // 2
    block = d_mixed.shape[2]
    scale = 1.0 / math.sqrt(HD)
    cos, sin = cosine[...], sine[...]
    for h in range(heads):
        d_key, d_value = [], []
        for q_at in range(0, LEN, wide):
            keys = q_at + wide
            query = qkv[h * HD : (h + 1) * HD, q_at:keys]
            key = qkv[part + h * HD : part + (h + 1) * HD, :keys]
            value = qkv[2 * part + h * HD : 2 * part + (h + 1) * HD, :keys]
            d_out = jnp.concatenate(
                [
                    d_mixed[q_at // block + b, h * HD : (h + 1) * HD, :]
                    for b in range(wide // block)
                ],
                axis=1,
            )
            scores = masked_scores(key, query, q_at)
            chances = jnp.exp(scores - log_total[h : h + 1, q_at:keys])
            d_chances = lax.dot_general(value, d_out, TN, preferred_element_type=F32)
            weighted = chances * d_chances
            inner = jnp.sum(weighted, axis=0, keepdims=True)
            d_scores = (weighted - chances * inner).astype(BF)
            grads[h * HD : (h + 1) * HD, q_at:keys] = (
                jnp.dot(key, d_scores, preferred_element_type=F32) * scale
            )
            d_key.append(lax.dot_general(query, d_scores, NT, preferred_element_type=F32))
            d_value.append(
                lax.dot_general(d_out, chances.astype(BF), NT, preferred_element_type=F32)
            )
        for base, items, factor in ((part, d_key, scale), (2 * part, d_value, 1.0)):
            at = base + h * HD
            grads[at : at + HD, :wide] = (items[0] + items[1][:, :wide]) * factor
            grads[at : at + HD, wide:] = items[1][:, wide:] * factor
    whole_grad = grads[...]
    pieces = []
    for kind in range(2):
        for h in range(heads):
            at = kind * part + h * HD
            low, high = whole_grad[at : at + half], whole_grad[at + half : at + ROT]
            pieces += [low * cos + high * sin, high * cos - low * sin]
            pieces.append(whole_grad[at + ROT : at + HD])
    pieces.append(whole_grad[2 * part :])
    result = jnp.concatenate(pieces, axis=0).astype(BF)
    for b in range(LEN // block):
        d_joined[b] = result[:, b * block : (b + 1) * block]


def gelu_both(hidden_in):
    normal_cdf = 0.5 * (1.0 + lax.erf(hidden_in * (1.0 / math.sqrt(2.0))))
    density = jnp.exp(-0.5 * hidden_in * hidden_in) * (1.0 / math.sqrt(2.0 * math.pi))
    return hidden_in * normal_cdf, normal_cdf + hidden_in * density


def widen_kernel(at, x, mat, bias, hidden, slope, turned):
    @pl.when(pl.program_id(0) == 0)
    def _():
        turned[...] = mat[:, at : at + turned.shape[0]].T

    hidden_in = jnp.dot(turned[...], x[0], preferred_element_type=F32) + column(bias[...])
    value, rise = gelu_both(hidden_in)
    hidden[0] = value.astype(BF)
    slope[0] = rise.astype(BF)


def branch_kernel(at, mixed, hidden, mat, out):
    cut = at + mixed.shape[1]
    out[0] = (
        jnp.dot(mat[:, at:cut], mixed[0], preferred_element_type=F32)
        + jnp.dot(mat[:, cut:], hidden[0], preferred_element_type=F32)
    ).astype(BF)


def narrow_kernel(at, grad, mat, slope, d_mixed, d_hidden, turned):
    @pl.when(pl.program_id(0) == 0)
    def _():
        turned[...] = mat[:, at:].T

    cut = d_mixed.shape[1]
    both = jnp.dot(turned[...], grad[0], preferred_element_type=F32)
    d_mixed[0] = both[:cut].astype(BF)
    d_hidden[0] = (both[cut:] * slope[0].astype(F32)).astype(BF)


def shaped_kernel(at, d_joined, d_hidden, qkv_mat, up_mat, out):
    cut, end = d_joined.shape[1], at + d_hidden.shape[1]
    out[0] = (
        jnp.dot(qkv_mat[:, :cut], d_joined[0], preferred_element_type=F32)
        + jnp.dot(up_mat[:, at:end], d_hidden[0], preferred_element_type=F32)
    ).astype(BF)


def lanes(ref):
    return jnp.concatenate([ref[b] for b in range(ref.shape[0])], axis=1)


def grad_kernel(pairs, sums, *refs):
    ins, out = refs[:-1], refs[-1]
    chunks = out.shape[0]
    rows = out.shape[1] - (EXTRA if sums else 0)
    lo = 0
    for left, right in pairs:
        width = ins[right].shape[1]
        got = lax.dot_general(
            lanes(ins[left]), lanes(ins[right]), NT, preferred_element_type=F32
        ).astype(BF)
        out[:, :rows, lo : lo + width] = got.reshape(chunks, rows, width)
        lo += width
    if sums:
        total = []
        for item in sums:
            right = lanes(ins[item])
            ones = jnp.ones((16, right.shape[1]), BF)
            total.append(lax.dot_general(ones, right, NT, preferred_element_type=F32)[:1])
        qkv_cols = ins[sums[0]].shape[1]
        used = sum(item.shape[1] for item in total)
        total = jnp.concatenate(total + [jnp.zeros((1, 4 * qkv_cols - used), F32)], axis=1)
        tail = [total[:, at : at + qkv_cols] for at in range(0, 4 * qkv_cols, qkv_cols)]
        tail = jnp.concatenate(tail + [jnp.zeros((EXTRA - 4, qkv_cols), F32)], axis=0).astype(BF)
        for c in range(chunks):
            out[c, rows:, :qkv_cols] = tail
            if out.shape[2] > qkv_cols:
                out[c, rows:, qkv_cols:] = jnp.zeros((EXTRA, out.shape[2] - qkv_cols), BF)


def finish_kernel(layer, split, norms, w_qkv, w_up, *refs):
    parts, outs = refs[: 1 + split], refs[-6:]
    d_qkv, d_up, d_dense, d_down, d_norm, sums = outs
    rows, qkv_cols = w_qkv.shape[1], w_qkv.shape[2]
    up_cols, mix_cols = w_up.shape[2], d_dense.shape[1]
    heads = qkv_cols // (3 * HD)
    got = parts[0][:rows, :qkv_cols].astype(F32)
    tail = parts[0][rows:, :qkv_cols].astype(F32)
    rest = parts[1][...] if split else parts[0][:rows, qkv_cols:].astype(F32)
    total = jnp.concatenate([tail[r : r + 1] for r in range(4)], axis=1)
    sums[0] = total
    gains = [column(norms[2 * layer + k : 2 * layer + k + 1, :]) for k in range(2)]
    shifts = [column(norms[4 + 2 * layer + k : 5 + 2 * layer + k, :]) for k in range(2)]
    raw = w_qkv[0].astype(F32)
    full = gains[0] * got + shifts[0] * total[:, :qkv_cols]
    gain_sum = jnp.zeros((rows, 1), F32)
    shift_sum = jnp.zeros((rows, 1), F32)
    for h in range(heads):
        for kind in range(3):
            to, at = (h * 3 + kind) * HD, (kind * heads + h) * HD
            d_qkv[0, :, to : to + HD] = full[:, at : at + HD]
            piece = raw[:, to : to + HD]
            gain_sum += jnp.sum(piece * got[:, at : at + HD], axis=1, keepdims=True)
            shift_sum += jnp.sum(piece * total[:, at : at + HD], axis=1, keepdims=True)
    up_sum = total[:, qkv_cols : qkv_cols + up_cols]
    raw = w_up[0].astype(F32)
    d_up[0] = gains[1] * rest[:, :up_cols] + shifts[1] * up_sum
    columns = [
        gain_sum,
        jnp.sum(raw * rest[:, :up_cols], axis=1, keepdims=True),
        shift_sum,
        jnp.sum(raw * up_sum, axis=1, keepdims=True),
        jnp.zeros((rows, 4), F32),
    ]
    d_norm[0] = jnp.transpose(jnp.concatenate(columns, axis=1))
    d_dense[0] = jnp.transpose(rest[:, up_cols : up_cols + mix_cols])
    d_down[0] = jnp.transpose(rest[:, up_cols + mix_cols :])


def normalize(resid):
    centered = resid - jnp.mean(resid, axis=-2, keepdims=True)
    factor = lax.rsqrt(jnp.mean(centered * centered, axis=-2, keepdims=True) + 1e-05)
    return (centered * factor, factor)


def by_head(mat):
    lead, cols = mat.shape[:-1], mat.shape[-1]
    mat = mat.reshape(lead + (3, cols // (3 * HD), HD))
    return jnp.swapaxes(mat, -3, -2).reshape(lead + (cols,))


def by_kind(mat):
    lead, cols = mat.shape[:-1], mat.shape[-1]
    mat = mat.reshape(lead + (cols // (3 * HD), 3, HD))
    return jnp.swapaxes(mat, -3, -2).reshape(lead + (cols,))


def per_device(
    tokens, cotangent, ln_gain, ln_bias, w_qkv, b_qkv, w_dense, b_dense, w_fc1, b_fc1, w_fc2, b_fc2
):
    token_count, model = tokens.shape
    rows = w_qkv.shape[1]
    qkv_cols, ff_cols = w_qkv.shape[2], w_fc1.shape[2]
    mix_cols = qkv_cols // 3
    in_cols, out_cols = qkv_cols + ff_cols, mix_cols + ff_cols
    blocks = lax.axis_size("tensor")
    block = token_count // blocks
    seqs, seq_blocks = token_count // LEN, LEN // block
    ring = Ring()
    count, me = ring.count, ring.me
    tables = rotate_tables()
    gains, shifts = ln_gain.astype(F32), ln_bias.astype(F32)

    small = 4 * qkv_cols
    own = jnp.concatenate(
        [
            by_kind(
                lax.dynamic_update_slice(
                    jnp.zeros((LAYERS, qkv_cols), F32),
                    b_qkv.astype(F32),
                    (0, me * b_qkv.shape[1]),
                )
            ),
            lax.dynamic_update_slice(
                jnp.zeros((LAYERS, ff_cols), F32), b_fc1.astype(F32), (0, me * b_fc1.shape[1])
            ),
            lax.dynamic_update_slice(
                jnp.zeros((LAYERS, small - in_cols), F32),
                b_dense.astype(F32) + b_fc2.astype(F32),
                (0, me * b_dense.shape[1]),
            ),
        ],
        axis=1,
    )
    norms = jnp.concatenate([gains.reshape(4, rows), shifts.reshape(4, rows)], axis=0)
    rest_cols = ff_cols + out_cols
    packed = call(
        pack_kernel,
        [
            shape((rows + EXTRA, qkv_cols)),
            shape((rows, rest_cols)),
            shape((rows, in_cols)),
            shape((rows, out_cols)),
        ],
        moved=8 * rows * (in_cols + out_cols),
    )(norms, own, w_qkv, w_fc1, w_dense, w_fc2)
    (qkv_0, tail), hops = ring.gather(packed[0], rows)
    mats = [[(qkv_0, 0)], []]
    tail = tail.reshape(LAYERS, 2, small)
    biases = tail[:, 0] + tail[:, 1]

    def turn(item):
        return jnp.swapaxes(item.reshape(blocks, block, item.shape[1]), 1, 2)

    def unturn(item):
        return jnp.swapaxes(item, 1, 2).reshape(token_count, model)

    def per_block(features):
        return pl.BlockSpec((1, features, block), lambda i: (i, 0, 0))

    def per_seq(features):
        return pl.BlockSpec((seq_blocks, features, block), lambda i: (i, 0, 0))

    def seq_lanes(features):
        return pl.BlockSpec((features, LEN), lambda i: (0, i))

    half_rot = ROT // 2
    block_of = lambda features: whole((blocks, features, block))

    def attend(normed, layer):
        mat, _ = mats[layer][0]
        return call(
            attend_kernel,
            [
                shape((qkv_cols, token_count)),
                shape((blocks, mix_cols, block)),
                shape((8, token_count), F32),
            ],
            grid=(seqs,),
            flops=2 * token_count * (model * qkv_cols + 2 * LEN * mix_cols),
            moved=2 * model * (token_count + qkv_cols),
            in_specs=[
                per_seq(model),
                whole((model, qkv_cols)),
                whole((1, qkv_cols)),
                whole((half_rot, LEN)),
                whole((half_rot, LEN)),
            ],
            out_specs=[seq_lanes(qkv_cols), per_seq(mix_cols), seq_lanes(8)],
            scratch_shapes=[pltpu.VMEM((qkv_cols, model), BF)],
        )(normed, mat, biases[layer : layer + 1, :qkv_cols], *tables)

    def widen(normed, layer):
        mat, at = mats[layer][1]
        return call(
            functools.partial(widen_kernel, at),
            [shape((blocks, ff_cols, block))] * 2,
            grid=(blocks,),
            flops=2 * token_count * model * ff_cols,
            moved=2 * model * (token_count + ff_cols) + 4 * token_count * ff_cols,
            in_specs=[per_block(model), whole(mat.shape), whole((1, ff_cols))],
            out_specs=[per_block(ff_cols)] * 2,
            scratch_shapes=[pltpu.VMEM((ff_cols, model), BF)],
        )(normed, mat, biases[layer : layer + 1, qkv_cols:in_cols])

    def branch_of(mixed, hidden, layer):
        mat, at = mats[layer][2]
        return call(
            functools.partial(branch_kernel, at),
            shape((blocks, model, block)),
            grid=(blocks,),
            flops=2 * token_count * model * out_cols,
            moved=2 * model * (token_count + out_cols) + 2 * token_count * out_cols,
            in_specs=[per_block(mix_cols), per_block(ff_cols), whole(mat.shape)],
            out_specs=per_block(model),
        )(mixed, hidden, mat)

    def narrow(grad_low, slope, layer):
        mat, at = mats[layer][2]
        return call(
            functools.partial(narrow_kernel, at),
            [shape((blocks, mix_cols, block)), shape((blocks, ff_cols, block))],
            grid=(blocks,),
            flops=2 * token_count * model * out_cols,
            moved=2 * model * (token_count + out_cols) + 4 * token_count * out_cols,
            in_specs=[per_block(model), whole(mat.shape), per_block(ff_cols)],
            out_specs=[per_block(mix_cols), per_block(ff_cols)],
            scratch_shapes=[pltpu.VMEM((out_cols, model), BF)],
        )(grad_low, mat, slope)

    def attend_back(qkv, log_total, d_mixed):
        return call(
            attend_back_kernel,
            shape((blocks, qkv_cols, block)),
            grid=(seqs,),
            flops=10 * token_count * LEN * mix_cols,
            moved=6 * token_count * qkv_cols,
            in_specs=[
                seq_lanes(qkv_cols),
                seq_lanes(8),
                per_seq(mix_cols),
                whole((half_rot, LEN)),
                whole((half_rot, LEN)),
            ],
            out_specs=per_seq(qkv_cols),
            scratch_shapes=[pltpu.VMEM((qkv_cols, LEN), F32)],
        )(qkv, log_total, d_mixed, *tables)

    def shaped_of(d_joined, d_hidden, layer):
        (qkv_mat, _), (up_mat, at) = mats[layer][:2]
        return call(
            functools.partial(shaped_kernel, at),
            shape((blocks, model, block)),
            grid=(blocks,),
            flops=2 * token_count * model * in_cols,
            moved=2 * model * (token_count + in_cols) + 2 * token_count * in_cols,
            in_specs=[
                per_block(qkv_cols),
                per_block(ff_cols),
                whole((model, qkv_cols)),
                whole(up_mat.shape),
            ],
            out_specs=per_block(model),
        )(d_joined, d_hidden, qkv_mat, up_mat)

    def grads_of(pairs, sums, *items):
        parts = 2
        lefts = {left for left, _ in pairs}
        cols = sum(items[right].shape[1] for _, right in pairs)
        high = rows + (EXTRA if sums else 0)
        return call(
            functools.partial(grad_kernel, pairs, sums),
            shape((count, high, cols)),
            grid=(parts,),
            flops=2 * token_count * model * cols,
            moved=2 * model * (token_count + cols) + 2 * token_count * cols,
            in_specs=[
                pl.BlockSpec((blocks, model // parts, block), lambda i: (0, i, 0))
                if k in lefts
                else block_of(item.shape[1])
                for k, item in enumerate(items)
            ],
            out_specs=pl.BlockSpec((count // parts, high, cols), lambda i: (i, 0, 0)),
        )(*items)

    def grad_step(grad, shaped, own_normed, factor):
        return grad + factor * (
            shaped
            - jnp.mean(shaped, axis=0, keepdims=True)
            - own_normed * jnp.mean(shaped * own_normed, axis=0, keepdims=True)
        )

    token_blocks = turn(tokens).astype(F32)
    resid_0 = tensor_own(token_blocks)
    own_normed_0, factor_0 = normalize(resid_0)
    normed_0 = normalize(token_blocks)[0].astype(BF)
    far = count // 2
    last = far - 1
    qkv_rows_0, mixed_0, log_0 = attend(normed_0, 0)
    (rest_0,), hops = ring.gather(packed[1], rows, hops[-1], {last: mixed_0})
    mats[0] += [(rest_0, 0), (rest_0, ff_cols)]
    hidden_0, slope_0 = widen(normed_0, 0)
    partial = branch_of(mixed_0, hidden_0, 0)
    (in_1,), hops = ring.gather(packed[2], rows, hops[max(last - 2, 0)], {last: partial})
    (out_1,), hops = ring.gather(packed[3], rows, hops[max(last - 2, 0)])
    mats[1] += [(in_1, 0), (in_1, qkv_cols), (out_1, 0)]
    branch, _ = tensor_scatter(partial)
    resid_1 = resid_0 + branch + biases[0, in_cols : in_cols + model][:, None]
    own_normed_1, factor_1 = normalize(resid_1)
    normed_1 = tensor_gather(own_normed_1.astype(BF))
    qkv_rows_1, mixed_1, log_1 = attend(normed_1, 1)
    hidden_1, slope_1 = widen(normed_1, 1)

    grad_low_2 = turn(cotangent)
    d_mixed, d_hidden = narrow(grad_low_2, slope_1, 1)
    d_joined = attend_back(qkv_rows_1, log_1, d_mixed)
    shaped, met = tensor_scatter(shaped_of(d_joined, d_hidden, 1))
    total_1 = grads_of(
        ((0, 2), (0, 3), (1, 4), (1, 5)),
        (2, 3, 6),
        after(normed_1, met),
        grad_low_2,
        d_joined,
        d_hidden,
        mixed_1,
        hidden_1,
        grad_low_2,
    )
    sum_1 = lax.psum_scatter(total_1, "shard", scatter_dimension=0, tiled=True)[0]
    grad_1 = grad_step(tensor_own(grad_low_2).astype(F32), shaped, own_normed_1, factor_1)
    own_low_1 = grad_1.astype(BF)
    grad_low_1 = tensor_gather(own_low_1)

    branch, _ = tensor_scatter(branch_of(mixed_1, after(hidden_1, total_1, own_low_1), 1))
    resid_2 = resid_1 + branch + biases[1, in_cols : in_cols + model][:, None]
    output = tensor_gather(resid_2.astype(BF))

    d_mixed, d_hidden = narrow(grad_low_1, slope_0, 0)
    rest_grads = grads_of(
        ((0, 2), (1, 3), (1, 4)), (), normed_0, grad_low_1, d_hidden, mixed_0, hidden_0
    )
    d_joined = attend_back(qkv_rows_0, log_0, after(d_mixed, rest_grads))
    qkv_grads = grads_of(((0, 1),), (1, 2, 3), normed_0, d_joined, d_hidden, grad_low_1)
    shaped, _ = tensor_scatter(shaped_of(after(d_joined, qkv_grads), d_hidden, 0))
    grad_0 = grad_step(grad_1, shaped, own_normed_0, factor_0)
    grad_low_0 = tensor_gather(grad_0.astype(BF))

    def finish(layer, parts, kept):
        def at(dims):
            return pl.BlockSpec((1,) + dims, lambda i: (layer, 0, 0))

        outs = [
            (rows, qkv_cols), (rows, ff_cols), w_dense.shape[1:], w_fc2.shape[1:], (8, rows),
            (1, small),
        ]
        first = 3 + len(parts)
        return call(
            functools.partial(finish_kernel, layer, len(parts) - 1),
            [shape((LAYERS,) + item, F32) for item in outs],
            grid=(1,),
            moved=8 * rows * (in_cols + out_cols),
            in_specs=[whole(norms.shape), at((rows, qkv_cols)), at((rows, ff_cols))]
            + [whole(item.shape) for item in parts]
            + [pl.BlockSpec(memory_space=pl.ANY)] * len(kept),
            out_specs=[at(item) for item in outs],
            input_output_aliases={first + k: k for k in range(len(kept))},
        )(norms, w_qkv, w_fc1, *parts, *kept)

    kept = finish(1, (sum_1,), ())
    rest_sum = ring.scatter(rest_grads)
    qkv_sum = ring.scatter(qkv_grads, kept[4])
    d_qkv, d_up, d_dense, d_down, d_norm, sums = finish(0, (qkv_sum, rest_sum), kept)
    d_norm = tensor_small_sum(d_norm)
    sums = sums[:, 0]
    d_out_bias = lax.dynamic_slice(
        sums, (0, in_cols + me * b_dense.shape[1]), b_dense.shape
    )
    return (
        unturn(output),
        unturn(grad_low_0),
        d_norm[:, :2],
        d_norm[:, 2:4],
        d_qkv,
        lax.dynamic_slice(by_head(sums[:, :qkv_cols]), (0, me * b_qkv.shape[1]), b_qkv.shape),
        d_dense,
        d_out_bias,
        d_up,
        lax.dynamic_slice(sums, (0, qkv_cols + me * b_fc1.shape[1]), b_fc1.shape),
        d_down,
        d_out_bias,
    )


def solution(mesh):
    in_specs = (
        P("shard", None),
        P("shard", None),
        P(None, None, "shard"),
        P(None, None, "shard"),
        P(None, "shard", "tensor"),
        P(None, ("tensor", "shard")),
        P(None, "tensor", "shard"),
        P(None, "shard"),
        P(None, "shard", "tensor"),
        P(None, ("tensor", "shard")),
        P(None, "tensor", "shard"),
        P(None, "shard"),
    )
    out_specs = (
        P("shard", None),
        P("shard", None),
        P(None, None, "shard"),
        P(None, None, "shard"),
        P(None, "shard", "tensor"),
        P(None, ("tensor", "shard")),
        P(None, "tensor", "shard"),
        P(None, "shard"),
        P(None, "shard", "tensor"),
        P(None, ("tensor", "shard")),
        P(None, "tensor", "shard"),
        P(None, "shard"),
    )
    return jax.shard_map(
        per_device, mesh=mesh, in_specs=in_specs, out_specs=out_specs, check_vma=False
    )
```
